256 devices in a mesh: row: 32 (over z, x_hi, core), col: 8 (over y, x_lo).
Axes of the slice: x: 4 (x_hi: 2, x_lo: 2; x = x_hi * 2 + x_lo), y: 4, z: 8, core: 2. Of those that a mesh axis runs over, the one named last changes fastest.
Arguments:
- s_matrix: bfloat16 [2, 16384, 32768], P(None, 'row', 'col'), may hold values from -0.046875 to 0.046875
- slab: bfloat16 [2, 32768, 384], P(None, ('col', 'row')), may hold values from -6 to 6
- beam_hkl: int32 [3, 32768], P(None, ('col', 'row')), may hold values from -24 to 24
Outputs:
- squared: bfloat16 [2, 16384, 384], P(None, 'row', 'col')
The draws below stay inside these ranges and needn't reach their ends.
All inputs are finite; a program needn't handle non-finite values.
Results may differ from the reference program's by a relative error of at most 0.014.
Values may be sent and summed in bfloat16 or wider, within the bound.
A program may use at most 64 MiB of HBM per device.

```python
import jax
import jax.numpy as jnp

N = 32768
C = 384
M = 16384


def set_ends(array, stream_key, least, largest):
    extent = array.shape
    index_at = [jax.random.randint(jax.random.fold_in(stream_key, axis), (), 0, extent[axis]) for axis in range(len(extent))]
    array = array.at[tuple(index_at)].set(least)
    longest = extent.index(max(extent))
    index_at[longest] = (index_at[longest] + 1) % extent[longest]
    return array.at[tuple(index_at)].set(largest)


def strengthened(drawn, rng, source, target, shards_of, factor):
    def block_of(axis_at):
        return (jnp.arange(drawn.shape[axis_at]) // (drawn.shape[axis_at] // shards_of)).reshape((-1,) + (1,) * (drawn.ndim - 1 - axis_at))

    one_side = jax.random.permutation(rng, shards_of)[block_of(target)]
    other_side = (block_of(target) + shards_of // 2) % shards_of
    return jnp.where((block_of(source) == one_side) | (block_of(source) == other_side), factor * drawn, drawn)


def steps_of(own_key, shape, shards, least, high):
    factor_of = 1.0
    for axis_at, blocks in shards:
        steps = jax.random.uniform(jax.random.fold_in(jax.random.fold_in(own_key, 6), axis_at), (blocks,), jnp.float32, least / len(shards), high / len(shards))
        factor_of = factor_of * jnp.repeat(jnp.exp(steps), shape[axis_at] // blocks).reshape((-1,) + (1,) * (len(shape) - 1 - axis_at))
    return factor_of


def gaussian(rng, extent, deviation, most, pieces=(), kind=jnp.bfloat16):
    result = deviation * jax.random.normal(rng, extent, jnp.float32)
    if pieces:
        result = result * steps_of(rng, extent, pieces, -0.22, 0.18)
    return jnp.clip(result, -most, most).astype(kind)


def heavy_noise(key, shape, width, most, pieces, heavy, dtype=jnp.bfloat16):
    array = width * jax.random.normal(key, shape, jnp.float32)
    if pieces:
        array = array * steps_of(key, shape, pieces, -0.22, 0.18)
    return jnp.clip(strengthened(array, jax.random.fold_in(key, 3), *heavy), -most, most).astype(dtype)


def setup_inputs(seed: int = 0) -> dict:
    key_list = jax.random.split(jax.random.key(seed), 4)
    return {
        "s_matrix": heavy_noise(key_list[0], (2, M, N), (2 * N) ** -0.5, 0.046875, ((1, 32), (2, 8)), (2, 1, 32, 2.75)),
        "slab": gaussian(key_list[1], (2, N, C), 1.0, 6.0, ((1, 256),)),
        "beam_hkl": set_ends(jax.random.randint(key_list[2], (3, N), -24, 25), jax.random.fold_in(key_list[2], 1), -24, 24).astype(jnp.int32),
    }


def reference(s_matrix, slab, beam_hkl):
    hkl_float = beam_hkl.astype(jnp.float32)
    angles = 0.61 * (hkl_float[0] * hkl_float[0] + hkl_float[1] * hkl_float[1] + hkl_float[2] * hkl_float[2]) + 0.29 * hkl_float[0] - 0.17 * hkl_float[1] + 0.43 * hkl_float[2]
    cosine = jnp.cos(angles)[:, None]
    sine = jnp.sin(angles)[:, None]
    slab_real = slab[0].astype(jnp.float32)
    slab_imag = slab[1].astype(jnp.float32)
    phased_real = (cosine * slab_real - sine * slab_imag).astype(jnp.bfloat16)
    phased_imag = (cosine * slab_imag + sine * slab_real).astype(jnp.bfloat16)
    part_real = jnp.dot(s_matrix[0], phased_real, preferred_element_type=jnp.float32) - jnp.dot(s_matrix[1], phased_imag, preferred_element_type=jnp.float32)
    part_imag = jnp.dot(s_matrix[0], phased_imag, preferred_element_type=jnp.float32) + jnp.dot(s_matrix[1], phased_real, preferred_element_type=jnp.float32)
    return jnp.stack([part_real, part_imag]).astype(jnp.bfloat16)
```

```python
import functools

import jax
import jax.numpy as jnp
from jax import lax
from jax.experimental import pallas as pl
from jax.experimental.pallas import tpu as pltpu
from jax.sharding import PartitionSpec as P

MESH = pl.DeviceIdType.MESH
PANELS = 3
OFFSETS = (0, 1, -1, 2, -2, 3, -3, 4)
WIRE = 1.37
CORE_WIRE = 0.2
LATENCY = {"zp": 1.7, "zm": 1.7, "x": 2.5, "c": 1.0}
BACKLOG = 1.0
COARSE = (
    ((0, 0), (0, 1), (0, -1), (1, 0)),
    ((0, 2), (0, -2), (1, 1), (1, -1)),
    ((0, 3), (0, -3), (1, 2), (1, -2)),
    ((0, 4), (1, 3), (1, -3), (1, 4)),
)
FINE = COARSE[:3] + (((0, 4),), ((1, 3), (1, -3)), ((1, 4),))
GROUPS = (COARSE, COARSE, FINE)


def arrivals(p):
    table = {(p, 1, 0, None): ("x", (p, 0, 0, None))}
    for s, link in ((1, "zm"), (-1, "zp")):
        near = 0 if s == 1 else 1
        for d in (1, 2, 3):
            table[(p, 0, s * d, None)] = (link, (p, 0, s * (d - 1), None))
        table[(p, 0, 4, near)] = (link, (p, 0, s * 3, near))
        table[(p, 1, s, None)] = (link, (p, 1, 0, None))
        table[(p, 1, 2 * s, 1 - near)] = (link, (p, 1, s, 1 - near))
        table[(p, 1, 2 * s, near)] = ("x", (p, 0, 2 * s, near))
        table[(p, 1, 3 * s, None)] = ("x", (p, 0, 3 * s, None))
        table[(p, 1, 4, near)] = ("x", (p, 0, 4, near))
    return table


def pieces(part):
    p, h, d, half = part
    split = (h, d) in ((0, 4), (1, 4), (1, 2), (1, -2))
    if not split:
        return [(p, h, d, None)]
    return [(p, h, d, half)] if half is not None else [(p, h, d, 0), (p, h, d, 1)]


def schedule():
    sends = []
    for p in range(PANELS):
        for dst, (link, src) in arrivals(p).items():
            sends.append((link, dst, src, WIRE * (1.0 if dst[3] is None else 0.5)))
        for h in (0, 1):
            for d in OFFSETS:
                sends.append(("c", (p, h, d, "c"), (p, h, d, None), CORE_WIRE))

    def depth(dst):
        if dst[3] == "c":
            return 0
        below = [depth(s[1]) for s in sends if s[0] != "c" and dst in pieces(s[2])]
        return 1 + max(below, default=0)

    rank = {s[1]: (s[1][0], -depth(s[1])) for s in sends}
    arrive = {(p, 0, 0, None): 0.0 for p in range(PANELS)}
    free = {link: 0.0 for link in LATENCY}
    products = [(p, g) for p in range(PANELS) for g in range(len(GROUPS[p]))]
    order, now = [], 0.0

    def here(part):
        return all(arrive.get(k, 1e9) <= now for k in pieces(part))

    while sends or products:
        moved = False
        for link in ("zm", "zp", "x", "c"):
            able = [s for s in sends if s[0] == link and here(s[2])]
            if able and (link == "c" or free[link] - now < BACKLOG):
                best = min(able, key=lambda s: rank[s[1]])
                free[link] = max(free[link], now) + best[3]
                arrive[best[1]] = free[link] + LATENCY[link]
                order.append(("send", best[1]))
                sends.remove(best)
                now += 0.03
                moved = True
        if moved:
            continue
        able = []
        for p, g in products:
            first = (p, g) == min(k for k in products if k[0] == p)
            blocks = GROUPS[p][g]
            if first and all(here((p, h, d, None)) and arrive.get((p, h, d, "c"), 1e9) <= now for h, d in blocks):
                able.append((p, g))
        if able:
            p, g = able[0]
            products.remove((p, g))
            order.append(("product", p, g))
            now += 0.1 + 0.19 * len(GROUPS[p][g])
            continue
        later = [a for a in arrive.values() if a > now]
        later += [f - BACKLOG + 1e-6 for f in free.values() if f - BACKLOG + 1e-6 > now]
        now = min(later)
    return order


def kernel(s_any, slab_any, hkl_any, out_ref, s_ref, slab_ref, hkl_ref, got, acc, part, ysum, yrecv, xsend, xrecv,
           s_sem, in_sem, send_sem, recv_sem, rs_send, rs_recv):
    row = lax.axis_index("row")
    col = lax.axis_index("col")
    z, xh, core = row // 4, (row // 2) % 2, row % 2
    y, xl = col // 2, col % 2
    peer = {
        "zp": ((z + 1) % 8 * 4 + xh * 2 + core, col),
        "zm": ((z + 7) % 8 * 4 + xh * 2 + core, col),
        "x": (z * 4 + (1 - xh) * 2 + core, col),
        "c": (z * 4 + xh * 2 + 1 - core, col),
        "y1": (row, (y + 1) % 4 * 2 + xl),
        "y2": (row, (y + 2) % 4 * 2 + xl),
        "y3": (row, (y + 3) % 4 * 2 + xl),
        "xn": (row, y * 2 + 1 - xl),
    }

    slab_copy = pltpu.make_async_copy(slab_any, slab_ref, in_sem.at[0])
    hkl_copy = pltpu.make_async_copy(hkl_any, hkl_ref, in_sem.at[1])
    s_copies = [pltpu.make_async_copy(s_any.at[i], s_ref.at[i], s_sem.at[i]) for i in range(2)]
    slab_copy.start()
    hkl_copy.start()
    for c in s_copies:
        c.start()

    barrier = pltpu.get_barrier_semaphore()
    for name in peer:
        pl.semaphore_signal(barrier, inc=1, device_id=peer[name], device_id_type=MESH)

    hkl_copy.wait()
    f = hkl_ref[...].astype(jnp.float32)
    h0, h1, h2 = f[0:1], f[1:2], f[2:3]
    angles = 0.61 * (h0 * h0 + h1 * h1 + h2 * h2) + 0.29 * h0 - 0.17 * h1 + 0.43 * h2
    cosine, sine = jnp.cos(angles), jnp.sin(angles)
    slab_copy.wait()
    re = jnp.transpose(slab_ref[0].astype(jnp.float32))
    im = jnp.transpose(slab_ref[1].astype(jnp.float32))
    phased = (
        (cosine * re - sine * im).astype(jnp.bfloat16),
        (cosine * im + sine * re).astype(jnp.bfloat16),
    )

    def slot(p, h, d, mine):
        return (p * 16 + h * 8 + OFFSETS.index(d)) * 2 + mine

    for p in range(PANELS):
        for o in range(8):
            for comp in range(2):
                at = o * 32 + comp * 16
                got[slot(p, 0, 0, 0), at:at + 16, :] = phased[comp][48 * o + 16 * p:48 * o + 16 * p + 16, :]

    table = {}
    for p in range(PANELS):
        table.update(arrivals(p))
        for h in (0, 1):
            for d in OFFSETS:
                table[(p, h, d, "c")] = ("c", (p, h, d, None))
    index = {dst: i for i, dst in enumerate(table)}

    def copy_to(dst):
        link, src = table[dst]
        half = dst[3]
        source = got.at[slot(*src[:3], 0)]
        target = got.at[slot(*dst[:3], 1 if half == "c" else 0)]
        if half in (0, 1):
            source = source.at[pl.ds(128 * half, 128)]
            target = target.at[pl.ds(128 * half, 128)]
        return pltpu.make_async_remote_copy(
            src_ref=source, dst_ref=target, send_sem=send_sem.at[index[dst]], recv_sem=recv_sem.at[index[dst]],
            device_id=peer[link], device_id_type=MESH,
        )

    seen = {(p, 0, 0, None) for p in range(PANELS)}

    def need(part_key):
        keys = [part_key] if part_key[3] == "c" else pieces(part_key)
        for k in keys:
            if k not in seen:
                seen.add(k)
                copy_to(k).wait_recv()

    def lhs_rhs(p, h, d, mine):
        block = got[slot(p, h, d, mine)]
        turned = jnp.concatenate(
            [t for o in range(8) for t in (-block[o * 32 + 16:o * 32 + 32], block[o * 32:o * 32 + 16])], axis=0
        )
        chip = (z + d + 8) % 8 * 2 + (xh if h == 0 else 1 - xh)
        beam = chip * 2 + (core if mine == 0 else 1 - core)
        columns = pl.ds(pl.multiple_of(beam * 128, 128), 128)
        return [block, turned], [s_ref[0, :, columns], s_ref[1, :, columns]]

    def product(p, g):
        left, right = [], []
        for h, d in GROUPS[p][g]:
            for mine in (0, 1):
                a, b = lhs_rhs(p, h, d, mine)
                left += a
                right += b
        return lax.dot_general(
            jnp.concatenate(left, axis=1), jnp.concatenate(right, axis=1), (((1,), (1,)), ((), ())),
            preferred_element_type=jnp.float32,
        )

    def y_copy(p, j):
        to = (y + j) % 4
        return pltpu.make_async_remote_copy(
            src_ref=part.at[p, pl.ds(pl.multiple_of(to * 64, 64), 64)], dst_ref=yrecv.at[p, j - 1],
            send_sem=rs_send.at[p * 4 + j - 1], recv_sem=rs_recv.at[p * 4 + j - 1],
            device_id=peer[f"y{j}"], device_id_type=MESH,
        )

    def x_copy(p):
        return pltpu.make_async_remote_copy(
            src_ref=xsend.at[p], dst_ref=xrecv.at[p], send_sem=rs_send.at[p * 4 + 3], recv_sem=rs_recv.at[p * 4 + 3],
            device_id=peer["xn"], device_id_type=MESH,
        )

    def scatter_y(p):
        for j in (2, 1, 3):
            y_copy(p, j).start()

    def scatter_x(p):
        for j in (2, 1, 3):
            y_copy(p, j).wait_recv()

        def total(which):
            rows = pl.ds(pl.multiple_of(which * 32, 32), 32)
            t = acc[p, pl.ds(pl.multiple_of(y * 64 + which * 32, 32), 32)]
            for j in range(3):
                t += yrecv[p, j, rows].astype(jnp.float32)
            return t

        xsend[p] = total(1 - xl).astype(jnp.bfloat16)
        x_copy(p).start()
        ysum[p] = total(xl)

    def finish(p):
        x_copy(p).wait_recv()
        t = (ysum[p] + xrecv[p].astype(jnp.float32)).astype(jnp.bfloat16)
        out_ref[0, 16 * p:16 * p + 16, :] = t[0:16]
        out_ref[1, 16 * p:16 * p + 16, :] = t[16:32]

    pl.semaphore_wait(barrier, len(peer))
    waiting = []
    loaded = False
    for step in schedule():
        if step[0] == "send":
            need(table[step[1]][1])
            copy_to(step[1]).start()
            continue
        _, p, g = step
        for h, d in GROUPS[p][g]:
            need((p, h, d, None))
            need((p, h, d, "c"))
        if not loaded:
            loaded = True
            for c in s_copies:
                c.wait()
        result = product(p, g)
        if g:
            result += acc[p]
        acc[p] = result
        if waiting and g == 1:
            scatter_x(waiting[0])
        if waiting and g == 2:
            finish(waiting.pop(0))
        if g == len(GROUPS[p]) - 1:
            part[p] = result.astype(jnp.bfloat16)
            scatter_y(p)
            waiting.append(p)
    for dst in table:
        copy_to(dst).wait_send()
    for p in waiting:
        scatter_x(p)
    for p in waiting:
        finish(p)
    for p in range(PANELS):
        for j in (1, 2, 3):
            y_copy(p, j).wait_send()
        x_copy(p).wait_send()


def per_device(s_matrix, slab, beam_hkl):
    rows = s_matrix.shape[1]
    n_copies = PANELS * (len(arrivals(0)) + 16)
    out = pl.pallas_call(
        kernel,
        out_shape=jax.ShapeDtypeStruct((2, 48, rows), jnp.bfloat16),
        in_specs=[pl.BlockSpec(memory_space=pl.ANY)] * 3,
        out_specs=pl.BlockSpec(memory_space=pltpu.VMEM),
        scratch_shapes=[
            pltpu.VMEM(s_matrix.shape, jnp.bfloat16),
            pltpu.VMEM(slab.shape, jnp.bfloat16),
            pltpu.VMEM(beam_hkl.shape, jnp.int32),
            pltpu.VMEM((PANELS * 32, 256, 128), jnp.bfloat16),
            pltpu.VMEM((PANELS, 256, rows), jnp.float32),
            pltpu.VMEM((PANELS, 256, rows), jnp.bfloat16),
            pltpu.VMEM((PANELS, 32, rows), jnp.float32),
            pltpu.VMEM((PANELS, 3, 64, rows), jnp.bfloat16),
            pltpu.VMEM((PANELS, 32, rows), jnp.bfloat16),
            pltpu.VMEM((PANELS, 32, rows), jnp.bfloat16),
            pltpu.SemaphoreType.DMA((2,)),
            pltpu.SemaphoreType.DMA((2,)),
            pltpu.SemaphoreType.DMA((n_copies,)),
            pltpu.SemaphoreType.DMA((n_copies,)),
            pltpu.SemaphoreType.DMA((PANELS * 4,)),
            pltpu.SemaphoreType.DMA((PANELS * 4,)),
        ],
        compiler_params=pltpu.CompilerParams(
            collective_id=0, has_side_effects=True, vmem_limit_bytes=48 * 2**20
        ),
        name="squared",
    )(s_matrix, slab, beam_hkl)
    return jnp.swapaxes(out, 1, 2)


def solution(mesh):
    placed = (P(None, "row", "col"), P(None, ("col", "row"), None), P(None, ("col", "row")))
    return jax.shard_map(
        per_device, mesh=mesh, in_specs=placed, out_specs=P(None, "row", "col"), check_vma=False
    )
```

```python
import jax
import jax.numpy as jnp
from jax import lax
from jax.experimental import pallas as pl
from jax.experimental.pallas import tpu as pltpu
from jax.sharding import PartitionSpec as P

MESH = pl.DeviceIdType.MESH
UNIT = 8
PANELS = ((0, 2), (2, 2), (4, 1), (5, 1))
DIRECT = (3,)
OFFSETS = (0, 1, -1, 2, -2, 3, -3, 4)
COARSE = (
    ((0, 0), (0, 1), (0, -1), (1, 0)),
    ((0, 2), (0, -2), (1, 1), (1, -1)),
    ((0, 3), (0, -3), (1, 2), (1, -2)),
    ((0, 4), (1, 3), (1, -3), (1, 4)),
)
FINE = COARSE[:3] + (((0, 4),), ((1, 3), (1, -3)), ((1, 4),))
GROUPS = (COARSE, COARSE, COARSE, FINE)

WIRE, CORE_WIRE = 0.69, 0.1
LATENCY = {"zm": 1.7, "zp": 1.7, "x": 2.5, "c": 1.0}
BACKLOG = 1.0


def arrivals(p):
    table = {(p, 1, 0, None): ("x", (p, 0, 0, None))}
    for s, link in ((1, "zm"), (-1, "zp")):
        near = 0 if s == 1 else 1
        for d in (1, 2, 3):
            table[(p, 0, s * d, None)] = (link, (p, 0, s * (d - 1), None))
        table[(p, 0, 4, near)] = (link, (p, 0, s * 3, near))
        table[(p, 1, s, None)] = ("x", (p, 0, s, None))
        table[(p, 1, 2 * s, None)] = (link, (p, 1, s, None))
        table[(p, 1, 3 * s, 1 - near)] = (link, (p, 1, 2 * s, 1 - near))
        table[(p, 1, 3 * s, near)] = ("x", (p, 0, 3 * s, near))
        table[(p, 1, 4, near)] = ("x", (p, 0, 4, near))
    return table


def copies():
    table = {}
    for p in range(len(PANELS)):
        table.update(arrivals(p))
        for h in (0, 1):
            for d in OFFSETS:
                table[(p, h, d, "c")] = ("c", (p, h, d, None))
    return table


def pieces(part, table):
    p, h, d, half = part
    if part in table or (h, d) == (0, 0):
        return [part]
    if half is None:
        return [(p, h, d, 0), (p, h, d, 1)]
    return pieces((p, h, d, None), table)


def schedule(table):
    sends = [(link, dst, pieces(src, table)) for dst, (link, src) in table.items()]

    def depth(dst):
        if dst[3] == "c":
            return 0
        return 1 + max([depth(s[1]) for s in sends if s[0] != "c" and dst in s[2]], default=0)

    rank = {s[1]: (s[1][0], -depth(s[1])) for s in sends}
    arrive = {(p, 0, 0, None): 0.0 for p in range(len(PANELS))}
    free = {link: 0.0 for link in LATENCY}
    products = [(p, g) for p in range(len(PANELS)) for g in range(len(GROUPS[p]))]
    later, order, now = [], [], 0.0
    while sends or products or later:
        moved = False
        for link in LATENCY:
            able = [s for s in sends if s[0] == link and all(arrive.get(k, 1e9) <= now for k in s[2])]
            if able and (link == "c" or free[link] - now < BACKLOG):
                best = min(able, key=lambda s: rank[s[1]])
                p, _, _, half = best[1]
                wire = PANELS[p][1] * (CORE_WIRE if link == "c" else WIRE * (1.0 if half is None else 0.5))
                free[link] = max(free[link], now) + wire
                arrive[best[1]] = free[link] + LATENCY[link]
                order.append(("send", best[1]))
                sends.remove(best)
                now += 0.03
                moved = True
        if moved:
            continue
        if later and later[0][0] <= now:
            _, op, p = later.pop(0)
            units = PANELS[p][1]
            order.append((op, p))
            now += 0.1 * units
            if op == "scatter_x":
                free["x"] = max(free["x"], now) + 0.35 * units
                later.append((free["x"] + 1.9, "finish", p))
                later.sort()
            continue
        if products:
            p, g = products[0]
            units = PANELS[p][1]
            parts = [k for h, d in GROUPS[p][g] for k in pieces((p, h, d, None), table) + [(p, h, d, "c")]]
            if all(arrive.get(k, 1e9) <= now for k in parts):
                products.pop(0)
                order.append(("product", p, g))
                now += 0.05 + (0.1 + 0.17 * len(GROUPS[p][g])) * units / 2
                if g == len(GROUPS[p]) - 1:
                    order.append(("scatter", p))
                    now += 0.1 * units
                    if p in DIRECT:
                        later.append((now + 1.35 * units + 3.4, "finish", p))
                    else:
                        later.append((now + 1.35 * units + 3.0, "scatter_x", p))
                    later.sort()
                continue
        events = list(arrive.values()) + [t[0] for t in later]
        events += [f - BACKLOG + 1e-6 for link, f in free.items() if any(s[0] == link for s in sends)]
        now = min(t for t in events if t > now)
    return order


def kernel(s_any, slab_any, hkl_any, out_ref, s_ref, slab_ref, hkl_ref, turned, got, acc, total, part, yrecv, drecv,
           ysum, xsend, xrecv, final, in_sem, send_sem, recv_sem, rs_send, rs_recv):
    row = lax.axis_index("row")
    col = lax.axis_index("col")
    z, xh, core = row // 4, (row // 2) % 2, row % 2
    y, xl = col // 2, col % 2
    rows = s_any.shape[1]
    peer = {
        "zp": ((z + 1) % 8 * 4 + xh * 2 + core, col),
        "zm": ((z + 7) % 8 * 4 + xh * 2 + core, col),
        "x": (z * 4 + (1 - xh) * 2 + core, col),
        "c": (z * 4 + xh * 2 + 1 - core, col),
    }
    owner = {(dy, dx): (y + dy) % 4 * 2 + (xl + dx) % 2 for dy in range(4) for dx in range(2) if dy or dx}
    owners = list(owner)
    for k in owner:
        peer[k] = (row, owner[k])

    slab_copy = pltpu.make_async_copy(slab_any, slab_ref, in_sem.at[0])
    hkl_copy = pltpu.make_async_copy(hkl_any, hkl_ref, in_sem.at[1])
    s_copies = [
        pltpu.make_async_copy(s_any.at[i], s_ref.at[pl.ds(i * rows, rows)], in_sem.at[2 + i]) for i in range(2)
    ]
    slab_copy.start()
    hkl_copy.start()
    barrier = pltpu.get_barrier_semaphore()
    for name in peer:
        pl.semaphore_signal(barrier, inc=1, device_id=peer[name], device_id_type=MESH)

    hkl_copy.wait()
    f = hkl_ref[...].astype(jnp.float32)
    h0, h1, h2 = f[0:1], f[1:2], f[2:3]
    angles = 0.61 * (h0 * h0 + h1 * h1 + h2 * h2) + 0.29 * h0 - 0.17 * h1 + 0.43 * h2
    cosine, sine = jnp.cos(angles), jnp.sin(angles)
    slab_copy.wait()
    for c in s_copies:
        c.start()
    for i in range(2):
        turned[i] = jnp.transpose(slab_ref[i].astype(jnp.float32))

    def slot(p, h, d, mine):
        first, units = PANELS[p]
        return first * 32 + ((h * 8 + OFFSETS.index(d)) * 2 + mine) * units

    def phase(p):
        first, units = PANELS[p]
        for u in range(units):
            for o in range(8):
                at = 48 * o + UNIT * (first + u)
                re, im = turned[0, at:at + UNIT], turned[1, at:at + UNIT]
                both = jnp.concatenate([cosine * re - sine * im, cosine * im + sine * re], axis=0)
                got[slot(p, 0, 0, 0) + u, 16 * o:16 * o + 16] = both.astype(jnp.bfloat16)

    table = copies()
    index = {dst: i for i, dst in enumerate(table)}

    def copy_to(dst):
        link, src = table[dst]
        half, units = dst[3], PANELS[dst[0]][1]

        def ref(part, mine):
            at = slot(*part[:3], mine)
            if half not in (0, 1):
                return got.at[pl.ds(at, units)]
            if units == 1:
                return got.at[at, pl.ds(64 * half, 64)]
            return got.at[pl.ds(at + half * units // 2, units // 2)]

        return pltpu.make_async_remote_copy(
            src_ref=ref(src, 0), dst_ref=ref(dst, 1 if half == "c" else 0),
            send_sem=send_sem.at[index[dst]], recv_sem=recv_sem.at[index[dst]],
            device_id=peer[link], device_id_type=MESH,
        )

    seen = set()

    def need(part_key):
        for k in pieces(part_key, table):
            if k in seen:
                continue
            seen.add(k)
            if k[1:] == (0, 0, None):
                phase(k[0])
            else:
                copy_to(k).wait_recv()

    def product(p, g):
        left, right = [], []
        units = PANELS[p][1]
        for h, d in GROUPS[p][g]:
            for mine in (0, 1):
                left.append(got[pl.ds(slot(p, h, d, mine), units)].reshape(units * 128, 128))
                chip = (z + d + 8) % 8 * 2 + (xh if h == 0 else 1 - xh)
                beam = chip * 2 + (core if mine == 0 else 1 - core)
                right.append(s_ref[:, pl.ds(pl.multiple_of(beam * 128, 128), 128)])
        result = lax.dot_general(
            jnp.concatenate(left, axis=1), jnp.concatenate(right, axis=1), (((1,), (1,)), ((), ())),
            preferred_element_type=jnp.float32,
        )
        size = pl.ds(0, units * 128)
        if g:
            result += acc[size]
        if g < len(GROUPS[p]) - 1:
            acc[size] = result
            return
        pairs = result.reshape(units * 8, 2, UNIT, 2 * rows)
        re, im = pairs[:, 0], pairs[:, 1]
        both = jnp.stack([re[..., :rows] - im[..., rows:], im[..., :rows] + re[..., rows:]], axis=1)
        both = both.reshape(units, 128, rows)
        mine = pl.ds(PANELS[p][0], units)
        total[mine] = both
        part[mine] = both.astype(jnp.bfloat16)

    def y_copy(p, j):
        to = (y + j) % 4
        mine = pl.ds(PANELS[p][0], PANELS[p][1])
        return pltpu.make_async_remote_copy(
            src_ref=part.at[mine, pl.ds(pl.multiple_of(to * 32, 32), 32)], dst_ref=yrecv.at[j - 1, mine],
            send_sem=rs_send.at[p * 8 + j], recv_sem=rs_recv.at[p * 8 + j],
            device_id=peer[(j, 0)], device_id_type=MESH,
        )

    def x_copy(p):
        mine = pl.ds(PANELS[p][0], PANELS[p][1])
        return pltpu.make_async_remote_copy(
            src_ref=xsend.at[mine], dst_ref=xrecv.at[mine], send_sem=rs_send.at[p * 8], recv_sem=rs_recv.at[p * 8],
            device_id=peer[(0, 1)], device_id_type=MESH,
        )

    def direct_copy(p, k):
        mine = pl.ds(PANELS[p][0], PANELS[p][1])
        i = owners.index(k)
        return pltpu.make_async_remote_copy(
            src_ref=part.at[mine, pl.ds(pl.multiple_of(owner[k] * 16, 16), 16)], dst_ref=drecv.at[i, mine],
            send_sem=rs_send.at[p * 8 + i], recv_sem=rs_recv.at[p * 8 + i],
            device_id=peer[k], device_id_type=MESH,
        )

    def scatter_copies(p):
        if p in DIRECT:
            return [direct_copy(p, k) for k in ((2, 1), (2, 0), (1, 1), (3, 1), (1, 0), (3, 0), (0, 1))]
        return [y_copy(p, j) for j in (2, 1, 3)]

    def scatter(p):
        for c in scatter_copies(p):
            c.start()

    def scatter_x(p):
        for c in scatter_copies(p):
            c.wait_recv()
        for u in range(PANELS[p][0], sum(PANELS[p])):
            for to in (1, 0):
                which = (xl + to) % 2
                t = total[u, pl.ds(pl.multiple_of(y * 32 + which * 16, 16), 16)]
                for j in range(3):
                    t += yrecv[j, u, pl.ds(pl.multiple_of(which * 16, 16), 16)].astype(jnp.float32)
                if to:
                    xsend[u] = t.astype(jnp.bfloat16)
                else:
                    ysum[u] = t
        x_copy(p).start()

    def finish(p):
        for c in scatter_copies(p) if p in DIRECT else [x_copy(p)]:
            c.wait_recv()
        for u in range(PANELS[p][0], sum(PANELS[p])):
            if p in DIRECT:
                t = total[u, pl.ds(pl.multiple_of(col * 16, 16), 16)]
                for i in range(len(owners)):
                    t += drecv[i, u].astype(jnp.float32)
            else:
                t = ysum[u] + xrecv[u].astype(jnp.float32)
            final[0, UNIT * u:UNIT * (u + 1)] = t[:UNIT]
            final[1, UNIT * u:UNIT * (u + 1)] = t[UNIT:]

    need((0, 0, 0, None))
    pl.semaphore_wait(barrier, len(peer))
    order = schedule(table)
    drained = max(i for i, step in enumerate(order) if step[0] == "scatter")
    loaded = False
    for i, step in enumerate(order):
        if step[0] == "send":
            need(table[step[1]][1])
            copy_to(step[1]).start()
        elif step[0] == "product":
            _, p, g = step
            for h, d in GROUPS[p][g]:
                need((p, h, d, None))
                need((p, h, d, "c"))
            if not loaded:
                loaded = True
                for c in s_copies:
                    c.wait()
            product(p, g)
        else:
            {"scatter": scatter, "scatter_x": scatter_x, "finish": finish}[step[0]](step[1])
        if i == drained:
            for dst in table:
                copy_to(dst).wait_send()
    out_ref[...] = final[...].astype(jnp.bfloat16)
    for p in range(len(PANELS)):
        for c in scatter_copies(p) + ([] if p in DIRECT else [x_copy(p)]):
            c.wait_send()


def per_device(s_matrix, slab, beam_hkl):
    rows, beams = s_matrix.shape[1:]
    units = sum(PANELS[-1])
    most = max(n for _, n in PANELS)
    n_copies = len(copies())
    out = pl.pallas_call(
        kernel,
        out_shape=jax.ShapeDtypeStruct((2, units * UNIT, rows), jnp.bfloat16),
        in_specs=[pl.BlockSpec(memory_space=pl.ANY)] * 3,
        out_specs=pl.BlockSpec(memory_space=pltpu.VMEM),
        scratch_shapes=[
            pltpu.VMEM((2 * rows, beams), jnp.bfloat16),
            pltpu.VMEM(slab.shape, jnp.bfloat16),
            pltpu.VMEM(beam_hkl.shape, jnp.int32),
            pltpu.VMEM((2, slab.shape[2], slab.shape[1]), jnp.float32),
            pltpu.VMEM((units * 32, 128, 128), jnp.bfloat16),
            pltpu.VMEM((most * 128, 2 * rows), jnp.float32),
            pltpu.VMEM((units, 128, rows), jnp.float32),
            pltpu.VMEM((units, 128, rows), jnp.bfloat16),
            pltpu.VMEM((3, units, 32, rows), jnp.bfloat16),
            pltpu.VMEM((7, units, 16, rows), jnp.bfloat16),
            pltpu.VMEM((units, 16, rows), jnp.float32),
            pltpu.VMEM((units, 16, rows), jnp.bfloat16),
            pltpu.VMEM((units, 16, rows), jnp.bfloat16),
            pltpu.VMEM((2, units * UNIT, rows), jnp.float32),
            pltpu.SemaphoreType.DMA((4,)),
            pltpu.SemaphoreType.DMA((n_copies,)),
            pltpu.SemaphoreType.DMA((n_copies,)),
            pltpu.SemaphoreType.DMA((len(PANELS) * 8,)),
            pltpu.SemaphoreType.DMA((len(PANELS) * 8,)),
        ],
        compiler_params=pltpu.CompilerParams(
            collective_id=0, has_side_effects=True, vmem_limit_bytes=62 * 2**20
        ),
        name="squared",
    )(s_matrix, slab, beam_hkl)
    return jnp.swapaxes(out, 1, 2)


def solution(mesh):
    placed = (P(None, "row", "col"), P(None, ("col", "row"), None), P(None, ("col", "row")))
    return jax.shard_map(
        per_device, mesh=mesh, in_specs=placed, out_specs=P(None, "row", "col"), check_vma=False
    )
```

```python
import jax
import jax.numpy as jnp
from jax import lax
from jax.experimental import pallas as pl
from jax.experimental.pallas import tpu as pltpu
from jax.sharding import PartitionSpec as P

MESH = pl.DeviceIdType.MESH
UNIT = 8
UNITS = 2
PANELS = 3
DIRECT = PANELS - 1
OFFSETS = (0, 1, -1, 2, -2, 3, -3, 4)
SIZE = (1, 2, 2, 2, 1)
OVER_Z = ({2: 1.0, 3: 0.5},) * PANELS
RANK = None

WIRE, CORE_WIRE, Y_WIRE = 0.69 * UNITS, 0.1 * UNITS, 1.375 * UNITS
LATENCY = {"z": 1.75, "x": 2.5, "c": 1.0}
BACKLOG = 0.5
LARGEST = 2


def transfers():
    table = []
    for p in range(PANELS):
        for e in (1, 2, 3, 4):
            table.append(("z", (p, 0, e, "z"), (p, 0, e - 1)))
        for e in range(5):
            share = OVER_Z[p].get(e, 0.0)
            if share > 0:
                table.append(("z", (p, 1, e, "z"), (p, 1, e - 1)))
            if share < 1:
                table.append(("x", (p, 1, e, "x"), (p, 0, e)))
        for h in (0, 1):
            for e in range(5):
                table.append(("c", (p, h, e, "c"), (p, h, e)))
    return table


def units_of(target):
    p, h, e, link = target
    if link == "c":
        return SIZE[e] * UNITS
    share = OVER_Z[p].get(e, 0.0) if h else 1.0
    if link == "z":
        return int(UNITS * share) if e < 4 else UNITS // 2
    return int(SIZE[e] * UNITS * (1 - share))


def schedule(table):
    targets = {t[1] for t in table}

    def parts(key):
        return [key + (link,) for link in ("z", "x") if key + (link,) in targets]

    def depth(key):
        return 1 + max([depth(t[1][:3]) for t in table if t[0] != "c" and t[2] == key], default=0)

    if RANK is None:
        rank = {t[1]: t[1][0] * 100 - (0 if t[0] == "c" else 10 * depth(t[1][:3])) for t in table}
    else:
        rank = {t[1]: r for t, r in zip(table, RANK)}
    waiting = {link: sorted((t for t in table if t[0] == link), key=lambda t: rank[t[1]]) for link in LATENCY}
    blocks = [(p, h, e) for p in range(PANELS) for e in range(5) for h in (0, 1)]
    free = {"z": 0.0, "x": 0.0, "c": 0.0, "y": 0.0}
    arrive, later, order, now = {}, [], [], 0.0
    while any(waiting.values()) or blocks or later:
        moved = False
        for link in waiting:
            if link != "c" and free[link] - now >= BACKLOG:
                continue
            for t in waiting[link]:
                if all(arrive.get(k, 1e9) <= now for k in parts(t[2])):
                    wire = units_of(t[1]) / UNITS * (CORE_WIRE if link == "c" else WIRE)
                    free[link] = max(free[link], now) + wire
                    arrive[t[1]] = free[link] + LATENCY[link]
                    order.append(("send", t))
                    waiting[link].remove(t)
                    now += 0.08 if link == "z" else 0.04
                    moved = True
                    break
        if moved:
            continue
        if later and later[0][0] <= now:
            _, op, p = later.pop(0)
            order.append((op, p))
            now += 0.05 * UNITS
            if op == "scatter_x":
                free["x"] = max(free["x"], now) + 0.35 * UNITS
                later.append((free["x"] + 1.9, "finish", p))
                later.sort()
            continue
        ready = [
            b for b in blocks if all(arrive.get(k, 1e9) <= now for k in parts(b)) and arrive.get(b + ("c",), 1e9) <= now
        ]
        if ready:
            p, n, job = min(b[0] for b in ready), 0, []
            for b in ready:
                if b[0] == p and (not job or n + SIZE[b[2]] <= LARGEST):
                    job.append(b)
                    n += SIZE[b[2]]
            for b in job:
                blocks.remove(b)
            last = all(b[0] != p for b in blocks)
            order.append(("product", p, tuple(b[1:] for b in job), last))
            now += 0.03 + 0.165 * n
            if last:
                now += 0.1 * UNITS
                order.append(("scatter", p))
                free["y"] = max(free["y"], now) + Y_WIRE
                if p == DIRECT:
                    free["x"] = max(free["x"], now) + Y_WIRE
                    later.append((max(free["y"] + 2.4, free["x"] + 2.9), "finish", p))
                else:
                    later.append((free["y"] + 2.2, "scatter_x", p))
                later.sort()
            continue
        events = list(arrive.values()) + [t[0] for t in later]
        events += [free[link] - BACKLOG + 1e-6 for link in ("z", "x") if waiting[link]]
        now = min(t for t in events if t > now)
    return order


def kernel(s_any, slab_any, hkl_any, out_ref, s_ref, slab_ref, hkl_ref, turned, got, acc, total, part, yrecv, drecv,
           ysum, xsend, xrecv, final, in_sem, send_sem, recv_sem, rs_send, rs_recv):
    row = lax.axis_index("row")
    col = lax.axis_index("col")
    z, xh, core = row // 4, (row // 2) % 2, row % 2
    y, xl = col // 2, col % 2
    rows = s_any.shape[1]
    peer = {
        "zp": ((z + 1) % 8 * 4 + xh * 2 + core, col),
        "zm": ((z + 7) % 8 * 4 + xh * 2 + core, col),
        "x": (z * 4 + (1 - xh) * 2 + core, col),
        "c": (z * 4 + xh * 2 + 1 - core, col),
    }
    owner = {(dy, dx): (y + dy) % 4 * 2 + (xl + dx) % 2 for dy in range(4) for dx in range(2) if dy or dx}
    owners = list(owner)
    for k in owner:
        peer[k] = (row, owner[k])

    slab_copy = pltpu.make_async_copy(slab_any, slab_ref, in_sem.at[0])
    hkl_copy = pltpu.make_async_copy(hkl_any, hkl_ref, in_sem.at[1])
    s_copies = [
        pltpu.make_async_copy(s_any.at[i], s_ref.at[pl.ds(i * rows, rows)], in_sem.at[2 + i]) for i in range(2)
    ]
    slab_copy.start()
    hkl_copy.start()
    barrier = pltpu.get_barrier_semaphore()
    for name in peer:
        pl.semaphore_signal(barrier, inc=1, device_id=peer[name], device_id_type=MESH)

    hkl_copy.wait()
    f = hkl_ref[...].astype(jnp.float32)
    h0, h1, h2 = f[0:1], f[1:2], f[2:3]
    angles = 0.61 * (h0 * h0 + h1 * h1 + h2 * h2) + 0.29 * h0 - 0.17 * h1 + 0.43 * h2
    cosine, sine = jnp.cos(angles), jnp.sin(angles)
    slab_copy.wait()
    for c in s_copies:
        c.start()
    for i in range(2):
        turned[i] = jnp.transpose(slab_ref[i].astype(jnp.float32))

    def slot(p, h, d, mine):
        return (p * 32 + mine * 16 + h * 8 + OFFSETS.index(d)) * UNITS

    def group(p, h, e, mine):
        return got.at[pl.ds(slot(p, h, e, mine), SIZE[e] * UNITS)]

    def phase(p):
        for u in range(UNITS):
            for o in range(8):
                at = 48 * o + UNIT * (p * UNITS + u)
                re, im = turned[0, at:at + UNIT], turned[1, at:at + UNIT]
                both = jnp.concatenate([cosine * re - sine * im, cosine * im + sine * re], axis=0)
                got[slot(p, 0, 0, 0) + u, 16 * o:16 * o + 16] = both.astype(jnp.bfloat16)

    table = transfers()
    signals = []
    for link, dst, _ in table:
        key = dst[:3] + (link == "c",)
        if key not in signals:
            signals.append(key)

    def move(p, at, to, size, link, key):
        return pltpu.make_async_remote_copy(
            src_ref=got.at[pl.ds(at, size)], dst_ref=got.at[pl.ds(to, size)],
            send_sem=send_sem.at[p], recv_sem=recv_sem.at[signals.index(key)],
            device_id=peer[link], device_id_type=MESH,
        )

    def moves(link, dst, src):
        p, h, e, _ = dst
        key = (p, h, e, link == "c")
        size = units_of(dst)
        if link == "c":
            return [move(p, slot(p, h, e, 0), slot(p, h, e, 1), size, "c", key)]
        if link == "x":
            skip = (SIZE[e] * UNITS - size) // 2
            return [move(p, slot(p, 0, e, 0) + skip, slot(p, 1, e, 0) + skip, size, "x", key)]
        both = []
        for s, way in ((1, "zm"), (-1, "zp")):
            skip = 0 if s == 1 else UNITS - size
            at = slot(p, h, s * (e - 1), 0) + skip
            to = slot(p, h, s * e if e < 4 else 4, 0) + skip
            both.append(move(p, at, to, size, way, key))
        return both

    seen = set()

    def need(p, h, e, twin):
        key = (p, h, e, twin)
        if key in seen:
            return
        seen.add(key)
        if key[1:] == (0, 0, False):
            phase(p)
            return
        ref = group(p, h, e, 1 if twin else 0)
        pltpu.make_async_remote_copy(
            src_ref=ref, dst_ref=ref, send_sem=send_sem.at[p], recv_sem=recv_sem.at[signals.index(key)],
            device_id=peer["c"], device_id_type=MESH,
        ).wait_recv()

    begun = set()

    def product(p, job, last):
        left, right = [], []
        for h, e in job:
            for d in (e, -e) if e in (1, 2, 3) else (e,):
                for mine in (0, 1):
                    left.append(got[pl.ds(slot(p, h, d, mine), UNITS)].reshape(UNITS * 128, 128))
                    chip = (z + d + 8) % 8 * 2 + (xh if h == 0 else 1 - xh)
                    beam = chip * 2 + (core if mine == 0 else 1 - core)
                    right.append(s_ref[:, pl.ds(pl.multiple_of(beam * 128, 128), 128)])
        result = lax.dot_general(
            jnp.concatenate(left, axis=1), jnp.concatenate(right, axis=1), (((1,), (1,)), ((), ())),
            preferred_element_type=jnp.float32,
        )
        if p in begun:
            result += acc[p]
        begun.add(p)
        if not last:
            acc[p] = result
            return
        pairs = result.reshape(UNITS * 8, 2, UNIT, 2 * rows)
        re, im = pairs[:, 0], pairs[:, 1]
        both = jnp.stack([re[..., :rows] - im[..., rows:], im[..., :rows] + re[..., rows:]], axis=1)
        both = both.reshape(UNITS, 128, rows)
        total[p] = both
        part[p] = both.astype(jnp.bfloat16)

    def y_copy(p, j):
        to = pl.ds(pl.multiple_of((y + j) % 4 * 32, 32), 32)
        return pltpu.make_async_remote_copy(
            src_ref=part.at[p, :, to], dst_ref=yrecv.at[p, j - 1],
            send_sem=rs_send.at[p], recv_sem=rs_recv.at[p], device_id=peer[(j, 0)], device_id_type=MESH,
        )

    def x_copy(p):
        return pltpu.make_async_remote_copy(
            src_ref=xsend.at[p], dst_ref=xrecv.at[p], send_sem=rs_send.at[PANELS + p], recv_sem=rs_recv.at[PANELS + p],
            device_id=peer[(0, 1)], device_id_type=MESH,
        )

    def direct_copy(p, k):
        to = pl.ds(pl.multiple_of(owner[k] * 16, 16), 16)
        return pltpu.make_async_remote_copy(
            src_ref=part.at[p, :, to], dst_ref=drecv.at[owners.index(k)],
            send_sem=rs_send.at[p], recv_sem=rs_recv.at[p], device_id=peer[k], device_id_type=MESH,
        )

    def scattered(p):
        ref = drecv if p == DIRECT else yrecv.at[p]
        return pltpu.make_async_remote_copy(
            src_ref=ref, dst_ref=ref, send_sem=rs_send.at[p], recv_sem=rs_recv.at[p],
            device_id=peer["c"], device_id_type=MESH,
        )

    def scatter(p):
        if p == DIRECT:
            for k in ((2, 1), (2, 0), (1, 1), (3, 1), (1, 0), (3, 0), (0, 1)):
                direct_copy(p, k).start()
        else:
            for j in (2, 1, 3):
                y_copy(p, j).start()

    def scatter_x(p):
        scattered(p).wait_recv()
        for to in (1, 0):
            which = (xl + to) % 2
            t = total[p, :, pl.ds(pl.multiple_of(y * 32 + which * 16, 16), 16)]
            for j in range(3):
                t += yrecv[p, j, :, pl.ds(pl.multiple_of(which * 16, 16), 16)].astype(jnp.float32)
            if to:
                xsend[p] = t.astype(jnp.bfloat16)
                x_copy(p).start()
            else:
                ysum[p] = t

    def finish(p):
        if p == DIRECT:
            scattered(p).wait_recv()
            t = total[p, :, pl.ds(pl.multiple_of(col * 16, 16), 16)]
            for i in range(len(owners)):
                t += drecv[i].astype(jnp.float32)
        else:
            x_copy(p).wait_recv()
            t = ysum[p] + xrecv[p].astype(jnp.float32)
        for u in range(UNITS):
            at = UNIT * (p * UNITS + u)
            final[0, at:at + UNIT] = t[u, :UNIT]
            final[1, at:at + UNIT] = t[u, UNIT:]

    need(0, 0, 0, False)
    pl.semaphore_wait(barrier, len(peer))
    order = schedule(table)
    drained = max(i for i, step in enumerate(order) if step[0] == "scatter")
    loaded = False
    for i, step in enumerate(order):
        if step[0] == "send":
            link, dst, src = step[1]
            need(*src, False)
            for c in moves(link, dst, src):
                c.start()
        elif step[0] == "product":
            _, p, job, last = step
            for h, e in job:
                need(p, h, e, False)
                need(p, h, e, True)
            if not loaded:
                loaded = True
                for c in s_copies:
                    c.wait()
            product(p, job, last)
        else:
            {"scatter": scatter, "scatter_x": scatter_x, "finish": finish}[step[0]](step[1])
        if i == drained:
            for p in range(PANELS):
                sent = sum(units_of(t[1]) * (2 if t[0] == "z" else 1) for t in table if t[1][0] == p)
                move(p, 0, 0, sent, "c", signals[0]).wait_send()
    out_ref[...] = final[...].astype(jnp.bfloat16)
    for p in range(PANELS):
        scattered(p).wait_send()
        if p != DIRECT:
            x_copy(p).wait_send()


def per_device(s_matrix, slab, beam_hkl):
    rows, beams = s_matrix.shape[1:]
    units = PANELS * UNITS
    n_signals = PANELS * 19
    out = pl.pallas_call(
        kernel,
        out_shape=pltpu.VMEM((2, units * UNIT, rows), jnp.bfloat16),
        in_specs=[pl.BlockSpec(memory_space=pltpu.HBM)] * 3,
        out_specs=pl.BlockSpec(memory_space=pltpu.VMEM),
        scratch_shapes=[
            pltpu.VMEM((2 * rows, beams), jnp.bfloat16),
            pltpu.VMEM(slab.shape, jnp.bfloat16),
            pltpu.VMEM(beam_hkl.shape, jnp.int32),
            pltpu.VMEM((2, slab.shape[2], slab.shape[1]), jnp.float32),
            pltpu.VMEM((units * 32, 128, 128), jnp.bfloat16),
            pltpu.VMEM((PANELS, UNITS * 128, 2 * rows), jnp.float32),
            pltpu.VMEM((PANELS, UNITS, 128, rows), jnp.float32),
            pltpu.VMEM((PANELS, UNITS, 128, rows), jnp.bfloat16),
            pltpu.VMEM((PANELS, 3, UNITS, 32, rows), jnp.bfloat16),
            pltpu.VMEM((7, UNITS, 16, rows), jnp.bfloat16),
            pltpu.VMEM((PANELS, UNITS, 16, rows), jnp.float32),
            pltpu.VMEM((PANELS, UNITS, 16, rows), jnp.bfloat16),
            pltpu.VMEM((PANELS, UNITS, 16, rows), jnp.bfloat16),
            pltpu.VMEM((2, units * UNIT, rows), jnp.float32),
            pltpu.SemaphoreType.DMA((4,)),
            pltpu.SemaphoreType.DMA((PANELS,)),
            pltpu.SemaphoreType.DMA((n_signals,)),
            pltpu.SemaphoreType.DMA((2 * PANELS,)),
            pltpu.SemaphoreType.DMA((2 * PANELS,)),
        ],
        compiler_params=pltpu.CompilerParams(
            collective_id=0, has_side_effects=True, vmem_limit_bytes=63 * 2**20
        ),
        name="squared",
    )(s_matrix, slab, beam_hkl)
    return jnp.swapaxes(out, 1, 2)


def solution(mesh):
    placed = (P(None, "row", "col"), P(None, ("col", "row"), None), P(None, ("col", "row")))
    return jax.shard_map(
        per_device, mesh=mesh, in_specs=placed, out_specs=P(None, "row", "col"), check_vma=False
    )
```

```python
import jax
import jax.numpy as jnp
from jax import lax
from jax.experimental import pallas as pl
from jax.experimental.pallas import tpu as pltpu
from jax.sharding import PartitionSpec as P

MESH = pl.DeviceIdType.MESH
UNIT = 8
UNITS = 2
PANELS = 3
DIRECT = (1, 2)
OFFSETS = (0, 1, -1, 2, -2, 3, -3, 4)
SIZE = (1, 2, 2, 2, 1)
OVER_Z = ({2: 1.0, 3: 0.5}, {1: 1.0, 3: 0.5}, {2: 1.0, 3: 0.5})
RANK = (
    -3174, -2803, -1957, -5707, 128, 2109, 1428, -980, -364, 1850, 410, 460, -1562, -3876, -3764, -1949,
    -605, 570, 1667, 718, 3137, 1407, -1062, 1151, 3079, 2229, -1576, 2413, 2506, -2405, 335, 258,
    -16, 4147, 315, -1335, 3264, 1811, -989, 908, 3207, -30, 1700, 349, 195, 933, 1704, 429,
    1786, 758, 2040, 3883, 1399, 17, 1124, 1720, -634, 2325, 3003, 3400,
)

WIRE, CORE_WIRE, Y_WIRE = 0.69 * UNITS, 0.1 * UNITS, 1.375 * UNITS
LATENCY = {"z": 2.1, "x": 2.7, "c": 0.9}
BACKLOG = 0.5
LARGEST = 4


def transfers():
    table = []
    for p in range(PANELS):
        for e in (1, 2, 3, 4):
            table.append(("z", (p, 0, e, "z"), (p, 0, e - 1)))
        for e in range(5):
            share = OVER_Z[p].get(e, 0.0)
            if share > 0:
                table.append(("z", (p, 1, e, "z"), (p, 1, e - 1)))
            if share < 1:
                table.append(("x", (p, 1, e, "x"), (p, 0, e)))
        for h in (0, 1):
            for e in range(5):
                table.append(("c", (p, h, e, "c"), (p, h, e)))
    return table


def units_of(target):
    p, h, e, link = target
    if link == "c":
        return SIZE[e] * UNITS
    share = OVER_Z[p].get(e, 0.0) if h else 1.0
    if link == "z":
        return int(UNITS * share) if e < 4 else UNITS // 2
    return int(SIZE[e] * UNITS * (1 - share))


def schedule(table):
    targets = {t[1] for t in table}

    def parts(key):
        return [key + (link,) for link in ("z", "x") if key + (link,) in targets]

    rank = {t[1]: r for t, r in zip(table, RANK)}
    waiting = {link: sorted((t for t in table if t[0] == link), key=lambda t: rank[t[1]]) for link in LATENCY}
    blocks = [(p, h, e) for p in range(PANELS) for e in range(5) for h in (0, 1)]
    free = {"z": 0.0, "x": 0.0, "c": 0.0, "y": 0.0}
    arrive, later, order, now = {}, [], [], 0.0
    while any(waiting.values()) or blocks or later:
        moved = False
        for link in waiting:
            if link != "c" and free[link] - now >= BACKLOG:
                continue
            for t in waiting[link]:
                if all(arrive.get(k, 1e9) <= now for k in parts(t[2])):
                    wire = units_of(t[1]) / UNITS * (CORE_WIRE if link == "c" else WIRE)
                    free[link] = max(free[link], now) + wire
                    arrive[t[1]] = free[link] + LATENCY[link]
                    order.append(("send", t))
                    waiting[link].remove(t)
                    now += 0.08 if link == "z" else 0.04
                    moved = True
                    break
        if moved:
            continue
        if later and later[0][0] <= now:
            _, op, p = later.pop(0)
            if op == "scatter_x":
                order.append((op, p))
            now += 0.05 * UNITS
            if op == "scatter_x":
                free["x"] = max(free["x"], now) + 0.35 * UNITS
                later.append((free["x"] + 1.9, "finish", p))
                later.sort()
            continue
        ready = [
            b for b in blocks if all(arrive.get(k, 1e9) <= now for k in parts(b)) and arrive.get(b + ("c",), 1e9) <= now
        ]
        if ready:
            p, n, job = min(b[0] for b in ready), 0, []
            for b in ready:
                if b[0] != p or (job and n + SIZE[b[2]] > LARGEST):
                    break
                job.append(b)
                n += SIZE[b[2]]
            for b in job:
                blocks.remove(b)
            last = all(b[0] != p for b in blocks)
            order.append(("product", p, tuple(b[1:] for b in job), last))
            now += 0.03 + 0.165 * n
            if last:
                now += 0.21
                order.append(("scatter", p))
                free["y"] = max(free["y"], now) + Y_WIRE
                if p in DIRECT:
                    free["x"] = max(free["x"], now) + Y_WIRE
                    later.append((max(free["y"] + 2.4, free["x"] + 2.9), "finish", p))
                else:
                    later.append((free["y"] + 2.2, "scatter_x", p))
                later.sort()
            continue
        events = list(arrive.values()) + [t[0] for t in later]
        events += [free[link] - BACKLOG + 1e-6 for link in ("z", "x") if waiting[link]]
        now = min(t for t in events if t > now)
    return order


def kernel(s_any, slab_any, hkl_any, out_ref, s_ref, slab_ref, hkl_ref, turned, got, acc, total, part, yrecv, drecv,
           ysum, xsend, xrecv, final, in_sem, send_sem, recv_sem, rs_send, rs_recv):
    row = lax.axis_index("row")
    col = lax.axis_index("col")
    z, xh, core = row // 4, (row // 2) % 2, row % 2
    y, xl = col // 2, col % 2
    rows = s_any.shape[1]
    peer = {
        "zp": ((z + 1) % 8 * 4 + xh * 2 + core, col),
        "zm": ((z + 7) % 8 * 4 + xh * 2 + core, col),
        "x": (z * 4 + (1 - xh) * 2 + core, col),
        "c": (z * 4 + xh * 2 + 1 - core, col),
    }
    owner = {(dy, dx): (y + dy) % 4 * 2 + (xl + dx) % 2 for dy in range(4) for dx in range(2) if dy or dx}
    owners = list(owner)
    for k in owner:
        peer[k] = (row, owner[k])

    slab_copy = pltpu.make_async_copy(slab_any, slab_ref, in_sem.at[0])
    hkl_copy = pltpu.make_async_copy(hkl_any, hkl_ref, in_sem.at[1])
    s_copies = [
        pltpu.make_async_copy(s_any.at[i], s_ref.at[pl.ds(i * rows, rows)], in_sem.at[2 + i]) for i in range(2)
    ]
    slab_copy.start()
    hkl_copy.start()
    barrier = pltpu.get_barrier_semaphore()
    for name in peer:
        pl.semaphore_signal(barrier, inc=1, device_id=peer[name], device_id_type=MESH)

    hkl_copy.wait()
    f = hkl_ref[...].astype(jnp.float32)
    h0, h1, h2 = f[0:1], f[1:2], f[2:3]
    angles = 0.61 * (h0 * h0 + h1 * h1 + h2 * h2) + 0.29 * h0 - 0.17 * h1 + 0.43 * h2
    cosine, sine = jnp.cos(angles), jnp.sin(angles)
    slab_copy.wait()
    for c in s_copies:
        c.start()
    for i in range(2):
        turned[i] = jnp.transpose(slab_ref[i].astype(jnp.float32))

    def slot(p, h, d, mine):
        return (p * 32 + mine * 16 + h * 8 + OFFSETS.index(d)) * UNITS

    def group(p, h, e, mine):
        return got.at[pl.ds(slot(p, h, e, mine), SIZE[e] * UNITS)]

    def phase(p):
        for u in range(UNITS):
            for o in range(8):
                at = 48 * o + UNIT * (p * UNITS + u)
                re, im = turned[0, at:at + UNIT], turned[1, at:at + UNIT]
                both = jnp.concatenate([cosine * re - sine * im, cosine * im + sine * re], axis=0)
                got[slot(p, 0, 0, 0) + u, 16 * o:16 * o + 16] = both.astype(jnp.bfloat16)

    table = transfers()
    signals = []
    for link, dst, _ in table:
        key = dst[:3] + (link == "c",)
        if key not in signals:
            signals.append(key)

    def move(p, at, to, size, link, key):
        return pltpu.make_async_remote_copy(
            src_ref=got.at[pl.ds(at, size)], dst_ref=got.at[pl.ds(to, size)],
            send_sem=send_sem.at[p], recv_sem=recv_sem.at[signals.index(key)],
            device_id=peer[link], device_id_type=MESH,
        )

    def moves(link, dst, src):
        p, h, e, _ = dst
        key = (p, h, e, link == "c")
        size = units_of(dst)
        if link == "c":
            return [move(p, slot(p, h, e, 0), slot(p, h, e, 1), size, "c", key)]
        if link == "x":
            skip = (SIZE[e] * UNITS - size) // 2
            return [move(p, slot(p, 0, e, 0) + skip, slot(p, 1, e, 0) + skip, size, "x", key)]
        both = []
        for s, way in ((1, "zm"), (-1, "zp")):
            skip = 0 if s == 1 else UNITS - size
            at = slot(p, h, s * (e - 1), 0) + skip
            to = slot(p, h, s * e if e < 4 else 4, 0) + skip
            both.append(move(p, at, to, size, way, key))
        return both

    seen = set()

    def need(p, h, e, twin):
        key = (p, h, e, twin)
        if key in seen:
            return
        seen.add(key)
        if key[1:] == (0, 0, False):
            phase(p)
            return
        ref = group(p, h, e, 1 if twin else 0)
        pltpu.make_async_remote_copy(
            src_ref=ref, dst_ref=ref, send_sem=send_sem.at[p], recv_sem=recv_sem.at[signals.index(key)],
            device_id=peer["c"], device_id_type=MESH,
        ).wait_recv()

    begun = set()

    def product(p, job, last):
        left, right = [], []
        for h, e in job:
            for d in (e, -e) if e in (1, 2, 3) else (e,):
                for mine in (0, 1):
                    left.append(got[pl.ds(slot(p, h, d, mine), UNITS)].reshape(UNITS * 128, 128))
                    chip = (z + d + 8) % 8 * 2 + (xh if h == 0 else 1 - xh)
                    beam = chip * 2 + (core if mine == 0 else 1 - core)
                    right.append(s_ref[:, pl.ds(pl.multiple_of(beam * 128, 128), 128)])
        result = lax.dot_general(
            jnp.concatenate(left, axis=1), jnp.concatenate(right, axis=1), (((1,), (1,)), ((), ())),
            preferred_element_type=jnp.float32,
        )
        if p in begun:
            result += acc[p]
        begun.add(p)
        if not last:
            acc[p] = result
            return
        pairs = result.reshape(UNITS * 8, 2, UNIT, 2 * rows)
        re, im = pairs[:, 0], pairs[:, 1]
        both = jnp.stack([re[..., :rows] - im[..., rows:], im[..., :rows] + re[..., rows:]], axis=1)
        both = both.reshape(UNITS, 128, rows)
        total[p] = both
        part[p] = both.astype(jnp.bfloat16)

    def y_copy(p, j):
        to = pl.ds(pl.multiple_of((y + j) % 4 * 32, 32), 32)
        return pltpu.make_async_remote_copy(
            src_ref=part.at[p, :, to], dst_ref=yrecv.at[p, j - 1],
            send_sem=rs_send.at[p], recv_sem=rs_recv.at[p], device_id=peer[(j, 0)], device_id_type=MESH,
        )

    def x_copy(p):
        return pltpu.make_async_remote_copy(
            src_ref=xsend.at[p], dst_ref=xrecv.at[p], send_sem=rs_send.at[PANELS + p], recv_sem=rs_recv.at[PANELS + p],
            device_id=peer[(0, 1)], device_id_type=MESH,
        )

    def direct_copy(p, k):
        to = pl.ds(pl.multiple_of(owner[k] * 16, 16), 16)
        return pltpu.make_async_remote_copy(
            src_ref=part.at[p, :, to], dst_ref=drecv.at[p, owners.index(k)],
            send_sem=rs_send.at[p], recv_sem=rs_recv.at[p], device_id=peer[k], device_id_type=MESH,
        )

    def scattered(p):
        ref = drecv.at[p] if p in DIRECT else yrecv.at[p]
        return pltpu.make_async_remote_copy(
            src_ref=ref, dst_ref=ref, send_sem=rs_send.at[p], recv_sem=rs_recv.at[p],
            device_id=peer["c"], device_id_type=MESH,
        )

    def scatter(p):
        if p in DIRECT:
            for k in ((2, 1), (2, 0), (1, 1), (3, 1), (1, 0), (3, 0), (0, 1)):
                direct_copy(p, k).start()
        else:
            for j in (2, 1, 3):
                y_copy(p, j).start()

    def scatter_x(p):
        scattered(p).wait_recv()
        for to in (1, 0):
            which = (xl + to) % 2
            t = total[p, :, pl.ds(pl.multiple_of(y * 32 + which * 16, 16), 16)]
            for j in range(3):
                t += yrecv[p, j, :, pl.ds(pl.multiple_of(which * 16, 16), 16)].astype(jnp.float32)
            if to:
                xsend[p] = t.astype(jnp.bfloat16)
                x_copy(p).start()
            else:
                ysum[p] = t

    def finish(p):
        if p in DIRECT:
            scattered(p).wait_recv()
            t = total[p, :, pl.ds(pl.multiple_of(col * 16, 16), 16)]
            for i in range(len(owners)):
                t += drecv[p, i].astype(jnp.float32)
        else:
            x_copy(p).wait_recv()
            t = ysum[p] + xrecv[p].astype(jnp.float32)
        for u in range(UNITS):
            at = UNIT * (p * UNITS + u)
            final[0, at:at + UNIT] = t[u, :UNIT]
            final[1, at:at + UNIT] = t[u, UNIT:]

    need(0, 0, 0, False)
    pl.semaphore_wait(barrier, len(peer))
    order = schedule(table)
    drained = max(i for i, step in enumerate(order) if step[0] == "scatter")
    loaded = False
    for i, step in enumerate(order):
        if step[0] == "send":
            link, dst, src = step[1]
            need(*src, False)
            for c in moves(link, dst, src):
                c.start()
        elif step[0] == "product":
            _, p, job, last = step
            for h, e in job:
                need(p, h, e, False)
                need(p, h, e, True)
            if not loaded:
                loaded = True
                for c in s_copies:
                    c.wait()
            product(p, job, last)
        else:
            {"scatter": scatter, "scatter_x": scatter_x}[step[0]](step[1])
        if i == drained:
            for p in range(PANELS):
                sent = sum(units_of(t[1]) * (2 if t[0] == "z" else 1) for t in table if t[1][0] == p)
                move(p, 0, 0, sent, "c", signals[0]).wait_send()
    for p in range(PANELS):
        finish(p)
    out_ref[...] = final[...].astype(jnp.bfloat16)
    for p in range(PANELS):
        scattered(p).wait_send()
        if p not in DIRECT:
            x_copy(p).wait_send()


def per_device(s_matrix, slab, beam_hkl):
    rows, beams = s_matrix.shape[1:]
    units = PANELS * UNITS
    n_signals = PANELS * 19
    out = pl.pallas_call(
        kernel,
        out_shape=pltpu.VMEM((2, units * UNIT, rows), jnp.bfloat16),
        in_specs=[pl.BlockSpec(memory_space=pltpu.HBM)] * 3,
        out_specs=pl.BlockSpec(memory_space=pltpu.VMEM),
        scratch_shapes=[
            pltpu.VMEM((2 * rows, beams), jnp.bfloat16),
            pltpu.VMEM(slab.shape, jnp.bfloat16),
            pltpu.VMEM(beam_hkl.shape, jnp.int32),
            pltpu.VMEM((2, slab.shape[2], slab.shape[1]), jnp.float32),
            pltpu.VMEM((units * 32, 128, 128), jnp.bfloat16),
            pltpu.VMEM((PANELS, UNITS * 128, 2 * rows), jnp.float32),
            pltpu.VMEM((PANELS, UNITS, 128, rows), jnp.float32),
            pltpu.VMEM((PANELS, UNITS, 128, rows), jnp.bfloat16),
            pltpu.VMEM((PANELS, 3, UNITS, 32, rows), jnp.bfloat16),
            pltpu.VMEM((PANELS, 7, UNITS, 16, rows), jnp.bfloat16),
            pltpu.VMEM((PANELS, UNITS, 16, rows), jnp.float32),
            pltpu.VMEM((PANELS, UNITS, 16, rows), jnp.bfloat16),
            pltpu.VMEM((PANELS, UNITS, 16, rows), jnp.bfloat16),
            pltpu.VMEM((2, units * UNIT, rows), jnp.float32),
            pltpu.SemaphoreType.DMA((4,)),
            pltpu.SemaphoreType.DMA((PANELS,)),
            pltpu.SemaphoreType.DMA((n_signals,)),
            pltpu.SemaphoreType.DMA((2 * PANELS,)),
            pltpu.SemaphoreType.DMA((2 * PANELS,)),
        ],
        compiler_params=pltpu.CompilerParams(
            collective_id=0, has_side_effects=True, vmem_limit_bytes=63 * 2**20
        ),
        name="squared",
    )(s_matrix, slab, beam_hkl)
    return jnp.swapaxes(out, 1, 2)


def solution(mesh):
    placed = (P(None, "row", "col"), P(None, ("col", "row"), None), P(None, ("col", "row")))
    return jax.shard_map(
        per_device, mesh=mesh, in_specs=placed, out_specs=P(None, "row", "col"), check_vma=False
    )
```

```python
import jax
import jax.numpy as jnp
from jax import lax
from jax.experimental import pallas as pl
from jax.experimental.pallas import tpu as pltpu
from jax.sharding import PartitionSpec as P

MESH = pl.DeviceIdType.MESH
UNIT = 8
PANELS = ((0, 1), (1, 2), (3, 2), (5, 1))
DIRECT = (2, 3)
OFFSETS = (0, 1, -1, 2, -2, 3, -3, 4)
SIZE = (1, 2, 2, 2, 1)
OVER_Z = ({2: 1.0, 4: 1.0}, {2: 1.0, 4: 1.0}, {2: 1.0, 3: 0.5}, {3: 1.0, 4: 1.0})
ORDER = (
    0, 42, 23, 28, 19, 38, 58, 5, 1, 4, 20, 10, 24, 39, 43, 2, 14, 21, 53, 68, 9, 49, 11, 15, 40, 6, 30, 29, 33, 7,
    59, 3, (0, ((1, 1), (0, 2))), 50, (0, ((0, 1),)), 26, 22, (2, ((0, 1),)), (2, ((1, 0),)), 12, (2, ((0, 2),)),
    34, 41, 44, (1, ((0, 1), (0, 0))), 31, 54, (0, ((0, 0), (0, 3))), 16, 51, 64, (1, ((1, 1),)), 8, 46, 13, 17,
    (1, ((0, 3),)), 25, (0, ((1, 2),)), (1, ((0, 2),)), 47, 48, (2, ((1, 1),)), 27, (3, ((0, 1),)), 52, 45, 62, 60,
    36, (0, ((0, 4),)), 63, 69, 18, (1, ((1, 0),)), (0, ((1, 3),)), 65, 32, 74, 67, (2, ((0, 0),)), (2, ((0, 4),)),
    35, (0, ((1, 0),)), (0, ((1, 4),)), 37, 55, (1, ((1, 3),)), (1, ((0, 4),)), (1, ((1, 2),)), 56, (1, ((1, 4),)),
    61, 70, 57, (2, ((1, 2),)), 72, 66, 75, (2, ((1, 3), (0, 3))), (2, ((1, 4),)), (3, ((0, 2),)), 73,
    (3, ((0, 0), (1, 0), (0, 3))), 71, (3, ((1, 2),)), 76, (0,), (3, ((1, 1), (1, 3))), (3, ((0, 4),)),
    (3, ((1, 4),)), (1,),
)


def transfers():
    table = []
    for p in range(len(PANELS)):
        for e in (1, 2, 3, 4):
            table.append(("z", (p, 0, e, "z"), (p, 0, e - 1)))
        for e in range(5):
            share = OVER_Z[p].get(e, 0.0)
            if share > 0:
                table.append(("z", (p, 1, e, "z"), (p, 1, e - 1)))
            if share < 1:
                table.append(("x", (p, 1, e, "x"), (p, 0, e)))
        for h in (0, 1):
            for e in range(5):
                table.append(("c", (p, h, e, "c"), (p, h, e)))
    return table


def halves_of(target):
    p, h, e, link = target
    halves = 2 * PANELS[p][1]
    if link == "c":
        return SIZE[e] * halves
    share = OVER_Z[p].get(e, 0.0) if h else 1.0
    if link == "z":
        return int(halves * share) if e < 4 else halves // 2
    return int(SIZE[e] * halves * (1 - share))


def kernel(s_any, slab_any, hkl_any, out_ref, s_ref, slab_ref, hkl_ref, turned, got, acc, total, part, yrecv, drecv,
           ysum, xsend, xrecv, final, in_sem, send_sem, recv_sem, rs_send, rs_recv):
    row = lax.axis_index("row")
    col = lax.axis_index("col")
    z, xh, core = row // 4, (row // 2) % 2, row % 2
    y, xl = col // 2, col % 2
    rows = s_any.shape[1]
    peer = {
        "zp": ((z + 1) % 8 * 4 + xh * 2 + core, col),
        "zm": ((z + 7) % 8 * 4 + xh * 2 + core, col),
        "x": (z * 4 + (1 - xh) * 2 + core, col),
        "c": (z * 4 + xh * 2 + 1 - core, col),
    }
    owner = {(dy, dx): (y + dy) % 4 * 2 + (xl + dx) % 2 for dy in range(4) for dx in range(2) if dy or dx}
    owners = list(owner)
    for k in owner:
        peer[k] = (row, owner[k])

    slab_copy = pltpu.make_async_copy(slab_any, slab_ref, in_sem.at[0])
    hkl_copy = pltpu.make_async_copy(hkl_any, hkl_ref, in_sem.at[1])
    s_copies = [
        pltpu.make_async_copy(s_any.at[i], s_ref.at[pl.ds(i * rows, rows)], in_sem.at[2 + i]) for i in range(2)
    ]
    slab_copy.start()
    hkl_copy.start()
    barrier = pltpu.get_barrier_semaphore()
    for name in peer:
        pl.semaphore_signal(barrier, inc=1, device_id=peer[name], device_id_type=MESH)

    hkl_copy.wait()
    f = hkl_ref[...].astype(jnp.float32)
    h0, h1, h2 = f[0:1], f[1:2], f[2:3]
    angles = 0.61 * (h0 * h0 + h1 * h1 + h2 * h2) + 0.29 * h0 - 0.17 * h1 + 0.43 * h2
    cosine, sine = jnp.cos(angles), jnp.sin(angles)
    slab_copy.wait()
    for c in s_copies:
        c.start()
    for i in range(2):
        turned[i] = jnp.transpose(slab_ref[i].astype(jnp.float32))

    def slot(p, h, d, mine):
        first, units = PANELS[p]
        return 2 * (first * 32 + (mine * 16 + h * 8 + OFFSETS.index(d)) * units)

    def group(p, h, e, mine):
        return got.at[pl.ds(slot(p, h, e, mine), SIZE[e] * 2 * PANELS[p][1])]

    def phase(p):
        first, units = PANELS[p]
        for u in range(units):
            for o in range(8):
                at = 48 * o + UNIT * (first + u)
                re, im = turned[0, at:at + UNIT], turned[1, at:at + UNIT]
                both = jnp.concatenate([cosine * re - sine * im, cosine * im + sine * re], axis=0)
                got[slot(p, 0, 0, 0) + 2 * u + o // 4, o % 4 * 16:o % 4 * 16 + 16] = both.astype(jnp.bfloat16)

    table = transfers()
    signals = []
    for link, dst, _ in table:
        key = dst[:3] + (link == "c",)
        if key not in signals:
            signals.append(key)

    def move(p, at, to, size, link, key):
        return pltpu.make_async_remote_copy(
            src_ref=got.at[pl.ds(at, size)], dst_ref=got.at[pl.ds(to, size)],
            send_sem=send_sem.at[p], recv_sem=recv_sem.at[signals.index(key)],
            device_id=peer[link], device_id_type=MESH,
        )

    def moves(link, dst, src):
        p, h, e, _ = dst
        key = (p, h, e, link == "c")
        size = halves_of(dst)
        if link == "c":
            return [move(p, slot(p, h, e, 0), slot(p, h, e, 1), size, "c", key)]
        if link == "x":
            skip = (SIZE[e] * 2 * PANELS[p][1] - size) // 2
            return [move(p, slot(p, 0, e, 0) + skip, slot(p, 1, e, 0) + skip, size, "x", key)]
        both = []
        for s, way in ((1, "zm"), (-1, "zp")):
            skip = 0 if s == 1 else 2 * PANELS[p][1] - size
            at = slot(p, h, s * (e - 1), 0) + skip
            to = slot(p, h, s * e if e < 4 else 4, 0) + skip
            both.append(move(p, at, to, size, way, key))
        return both

    seen = set()

    def need(p, h, e, twin):
        key = (p, h, e, twin)
        if key in seen:
            return
        seen.add(key)
        if key[1:] == (0, 0, False):
            phase(p)
            return
        ref = group(p, h, e, 1 if twin else 0)
        pltpu.make_async_remote_copy(
            src_ref=ref, dst_ref=ref, send_sem=send_sem.at[p], recv_sem=recv_sem.at[signals.index(key)],
            device_id=peer["c"], device_id_type=MESH,
        ).wait_recv()

    def panel(p):
        return pl.ds(*PANELS[p])

    begun = set()

    def product(p, job, last):
        left, right = [], []
        first, units = PANELS[p]
        for h, e in job:
            for d in (e, -e) if e in (1, 2, 3) else (e,):
                for mine in (0, 1):
                    left.append(got[pl.ds(slot(p, h, d, mine), 2 * units)].reshape(units * 128, 128))
                    chip = (z + d + 8) % 8 * 2 + (xh if h == 0 else 1 - xh)
                    beam = chip * 2 + (core if mine == 0 else 1 - core)
                    right.append(s_ref[:, pl.ds(pl.multiple_of(beam * 128, 128), 128)])
        result = lax.dot_general(
            jnp.concatenate(left, axis=1), jnp.concatenate(right, axis=1), (((1,), (1,)), ((), ())),
            preferred_element_type=jnp.float32,
        )
        mine = pl.ds(first * 128, units * 128)
        if p in begun:
            result += acc[mine]
        begun.add(p)
        if not last:
            acc[mine] = result
            return
        pairs = result.reshape(units * 8, 2, UNIT, 2 * rows)
        re, im = pairs[:, 0], pairs[:, 1]
        both = jnp.stack([re[..., :rows] - im[..., rows:], im[..., :rows] + re[..., rows:]], axis=1)
        both = both.reshape(units, 128, rows)
        total[panel(p)] = both
        part[panel(p)] = both.astype(jnp.bfloat16)

    def y_copy(p, j):
        to = pl.ds(pl.multiple_of((y + j) % 4 * 32, 32), 32)
        return pltpu.make_async_remote_copy(
            src_ref=part.at[panel(p), to], dst_ref=yrecv.at[j - 1, panel(p)],
            send_sem=rs_send.at[p], recv_sem=rs_recv.at[p], device_id=peer[(j, 0)], device_id_type=MESH,
        )

    def x_copy(p):
        return pltpu.make_async_remote_copy(
            src_ref=xsend.at[panel(p)], dst_ref=xrecv.at[panel(p)],
            send_sem=rs_send.at[len(PANELS) + p], recv_sem=rs_recv.at[len(PANELS) + p],
            device_id=peer[(0, 1)], device_id_type=MESH,
        )

    def direct_copy(p, k):
        to = pl.ds(pl.multiple_of(owner[k] * 16, 16), 16)
        return pltpu.make_async_remote_copy(
            src_ref=part.at[panel(p), to], dst_ref=drecv.at[owners.index(k), panel(p)],
            send_sem=rs_send.at[p], recv_sem=rs_recv.at[p], device_id=peer[k], device_id_type=MESH,
        )

    def scattered(p):
        ref = (drecv if p in DIRECT else yrecv).at[:, panel(p)]
        return pltpu.make_async_remote_copy(
            src_ref=ref, dst_ref=ref, send_sem=rs_send.at[p], recv_sem=rs_recv.at[p],
            device_id=peer["c"], device_id_type=MESH,
        )

    def scatter(p):
        if p in DIRECT:
            for k in ((2, 1), (2, 0), (1, 1), (3, 1), (1, 0), (3, 0), (0, 1)):
                direct_copy(p, k).start()
        else:
            for j in (2, 1, 3):
                y_copy(p, j).start()

    def scatter_x(p):
        scattered(p).wait_recv()
        for to in (1, 0):
            which = (xl + to) % 2
            t = total[panel(p), pl.ds(pl.multiple_of(y * 32 + which * 16, 16), 16)]
            for j in range(3):
                t += yrecv[j, panel(p), pl.ds(pl.multiple_of(which * 16, 16), 16)].astype(jnp.float32)
            if to:
                xsend[panel(p)] = t.astype(jnp.bfloat16)
                x_copy(p).start()
            else:
                ysum[panel(p)] = t

    def finish(p):
        if p in DIRECT:
            scattered(p).wait_recv()
            t = total[panel(p), pl.ds(pl.multiple_of(col * 16, 16), 16)]
            for i in range(len(owners)):
                t += drecv[i, panel(p)].astype(jnp.float32)
        else:
            x_copy(p).wait_recv()
            t = ysum[panel(p)] + xrecv[panel(p)].astype(jnp.float32)
        first, units = PANELS[p]
        for u in range(units):
            at = UNIT * (first + u)
            final[0, at:at + UNIT] = t[u, :UNIT]
            final[1, at:at + UNIT] = t[u, UNIT:]

    need(0, 0, 0, False)
    pl.semaphore_wait(barrier, len(peer))
    todo = {p: 10 for p in range(len(PANELS))}
    loaded = False
    for step in ORDER:
        if isinstance(step, int):
            link, dst, src = table[step]
            need(*src, False)
            for c in moves(link, dst, src):
                c.start()
        elif len(step) == 2:
            p, job = step
            for h, e in job:
                need(p, h, e, False)
                need(p, h, e, True)
            if not loaded:
                loaded = True
                for c in s_copies:
                    c.wait()
            todo[p] -= len(job)
            product(p, job, todo[p] == 0)
            if todo[p] == 0:
                scatter(p)
        else:
            scatter_x(step[0])
    for p in range(len(PANELS)):
        sent = sum(halves_of(t[1]) * (2 if t[0] == "z" else 1) for t in table if t[1][0] == p)
        move(p, 0, 0, sent, "c", signals[0]).wait_send()
    for p in range(len(PANELS)):
        finish(p)
    out_ref[...] = final[...].astype(jnp.bfloat16)
    for p in range(len(PANELS)):
        scattered(p).wait_send()
        if p not in DIRECT:
            x_copy(p).wait_send()


def per_device(s_matrix, slab, beam_hkl):
    rows, beams = s_matrix.shape[1:]
    units = sum(PANELS[-1])
    n_signals = len(PANELS) * 19
    out = pl.pallas_call(
        kernel,
        out_shape=pltpu.VMEM((2, units * UNIT, rows), jnp.bfloat16),
        in_specs=[pl.BlockSpec(memory_space=pltpu.HBM)] * 3,
        out_specs=pl.BlockSpec(memory_space=pltpu.VMEM),
        scratch_shapes=[
            pltpu.VMEM((2 * rows, beams), jnp.bfloat16),
            pltpu.VMEM(slab.shape, jnp.bfloat16),
            pltpu.VMEM(beam_hkl.shape, jnp.int32),
            pltpu.VMEM((2, slab.shape[2], slab.shape[1]), jnp.float32),
            pltpu.VMEM((units * 64, 64, 128), jnp.bfloat16),
            pltpu.VMEM((units * 128, 2 * rows), jnp.float32),
            pltpu.VMEM((units, 128, rows), jnp.float32),
            pltpu.VMEM((units, 128, rows), jnp.bfloat16),
            pltpu.VMEM((3, units, 32, rows), jnp.bfloat16),
            pltpu.VMEM((7, units, 16, rows), jnp.bfloat16),
            pltpu.VMEM((units, 16, rows), jnp.float32),
            pltpu.VMEM((units, 16, rows), jnp.bfloat16),
            pltpu.VMEM((units, 16, rows), jnp.bfloat16),
            pltpu.VMEM((2, units * UNIT, rows), jnp.float32),
            pltpu.SemaphoreType.DMA((4,)),
            pltpu.SemaphoreType.DMA((len(PANELS),)),
            pltpu.SemaphoreType.DMA((n_signals,)),
            pltpu.SemaphoreType.DMA((2 * len(PANELS),)),
            pltpu.SemaphoreType.DMA((2 * len(PANELS),)),
        ],
        compiler_params=pltpu.CompilerParams(
            collective_id=0, has_side_effects=True, vmem_limit_bytes=63 * 2**20
        ),
        name="squared",
    )(s_matrix, slab, beam_hkl)
    return jnp.swapaxes(out, 1, 2)


def solution(mesh):
    placed = (P(None, "row", "col"), P(None, ("col", "row"), None), P(None, ("col", "row")))
    return jax.shard_map(
        per_device, mesh=mesh, in_specs=placed, out_specs=P(None, "row", "col"), check_vma=False
    )
```

```python
import jax
import jax.numpy as jnp
from jax import lax
from jax.experimental import pallas as pl
from jax.experimental.pallas import tpu as pltpu
from jax.sharding import PartitionSpec as P

MESH = pl.DeviceIdType.MESH
UNIT = 8
PANELS = ((0, 2), (2, 2), (4, 2))
DIRECT = (1, 2)
OFFSETS = (0, 1, -1, 2, -2, 3, -3, 4)
SIZE = (1, 2, 2, 2, 1)
OVER_Z = ({2: 1.0, 3: 0.5}, {2: 1.0, 4: 1.0}, {1: 1.0, 2: 0.5})
ORDER = (
    0, 24, 4, 20, 39, 5, 1, 10, 25, 21, 34, 40, 43, 11, 12, 50, 49, 2, 22, 31, 46, 6, 16, (2, ((0, 1),)), 15, 8, 3,
    41, 27, (0, ((1, 1),)), 23, 32, (0, ((0, 1),)), 13, 29, (1, ((0, 2),)), 54, 7, (1, ((0, 3),)), 35, 30, 14, 44,
    9, (0, ((0, 2),)), 51, (1, ((0, 0),)), 42, 26, (0, ((0, 3),)), 47, 52, (1, ((1, 1),)), (2, ((1, 0),)), 33, 17,
    (0, ((0, 0), (1, 0))), (0, ((0, 4),)), 18, (1, ((0, 1),)), 28, (1, ((1, 0),)), 45, 19, 55, 37, 48,
    (0, ((1, 3),)), (0, ((1, 2),)), (0, ((1, 4),)), 36, (1, ((0, 4),)), (2, ((1, 1),)), 38, (1, ((1, 3),)), 53,
    (1, ((1, 2),)), 56, (1, ((1, 4),)), 57, (2, ((0, 2), (0, 3))), 58, (2, ((0, 4),)), (2, ((1, 2),)),
    (2, ((1, 3), (0, 0))), (2, ((1, 4),)), (0,),
)


def transfers():
    table = []
    for p in range(len(PANELS)):
        for e in (1, 2, 3, 4):
            table.append(("z", (p, 0, e, "z"), (p, 0, e - 1)))
        for e in range(5):
            share = OVER_Z[p].get(e, 0.0)
            if share > 0:
                table.append(("z", (p, 1, e, "z"), (p, 1, e - 1)))
            if share < 1:
                table.append(("x", (p, 1, e, "x"), (p, 0, e)))
        for h in (0, 1):
            for e in range(5):
                table.append(("c", (p, h, e, "c"), (p, h, e)))
    return table


def halves_of(target):
    p, h, e, link = target
    halves = 2 * PANELS[p][1]
    if link == "c":
        return SIZE[e] * halves
    share = OVER_Z[p].get(e, 0.0) if h else 1.0
    if link == "z":
        return int(halves * share) if e < 4 else halves // 2
    return int(SIZE[e] * halves * (1 - share))


def kernel(s_any, slab_any, hkl_any, out_ref, s_ref, slab_ref, hkl_ref, turned, got, acc, total, part, yrecv, drecv,
           ysum, xsend, xrecv, final, in_sem, send_sem, recv_sem, rs_send, rs_recv):
    row = lax.axis_index("row")
    col = lax.axis_index("col")
    z, xh, core = row // 4, (row // 2) % 2, row % 2
    y, xl = col // 2, col % 2
    rows = s_any.shape[1]
    peer = {
        "zp": ((z + 1) % 8 * 4 + xh * 2 + core, col),
        "zm": ((z + 7) % 8 * 4 + xh * 2 + core, col),
        "x": (z * 4 + (1 - xh) * 2 + core, col),
        "c": (z * 4 + xh * 2 + 1 - core, col),
    }
    owner = {(dy, dx): (y + dy) % 4 * 2 + (xl + dx) % 2 for dy in range(4) for dx in range(2) if dy or dx}
    owners = list(owner)
    for k in owner:
        peer[k] = (row, owner[k])

    slab_copy = pltpu.make_async_copy(slab_any, slab_ref, in_sem.at[0])
    hkl_copy = pltpu.make_async_copy(hkl_any, hkl_ref, in_sem.at[1])
    s_copies = [
        pltpu.make_async_copy(s_any.at[i], s_ref.at[pl.ds(i * rows, rows)], in_sem.at[2 + i]) for i in range(2)
    ]
    slab_copy.start()
    hkl_copy.start()
    barrier = pltpu.get_barrier_semaphore()
    for name in peer:
        pl.semaphore_signal(barrier, inc=1, device_id=peer[name], device_id_type=MESH)

    hkl_copy.wait()
    f = hkl_ref[...].astype(jnp.float32)
    h0, h1, h2 = f[0:1], f[1:2], f[2:3]
    angles = 0.61 * (h0 * h0 + h1 * h1 + h2 * h2) + 0.29 * h0 - 0.17 * h1 + 0.43 * h2
    cosine, sine = jnp.cos(angles), jnp.sin(angles)
    slab_copy.wait()
    for c in s_copies:
        c.start()
    for i in range(2):
        turned[i] = jnp.transpose(slab_ref[i].astype(jnp.float32))

    def slot(p, h, d, mine):
        first, units = PANELS[p]
        return 2 * (first * 32 + (mine * 16 + h * 8 + OFFSETS.index(d)) * units)

    def group(p, h, e, mine):
        return got.at[pl.ds(slot(p, h, e, mine), SIZE[e] * 2 * PANELS[p][1])]

    def phase(p):
        first, units = PANELS[p]
        for u in range(units):
            for o in range(8):
                at = 48 * o + UNIT * (first + u)
                re, im = turned[0, at:at + UNIT], turned[1, at:at + UNIT]
                both = jnp.concatenate([cosine * re - sine * im, cosine * im + sine * re], axis=0)
                got[slot(p, 0, 0, 0) + 2 * u + o // 4, o % 4 * 16:o % 4 * 16 + 16] = both.astype(jnp.bfloat16)

    table = transfers()
    signals = []
    for link, dst, _ in table:
        key = dst[:3] + (link == "c",)
        if key not in signals:
            signals.append(key)

    def move(p, at, to, size, link, key):
        return pltpu.make_async_remote_copy(
            src_ref=got.at[pl.ds(at, size)], dst_ref=got.at[pl.ds(to, size)],
            send_sem=send_sem.at[p], recv_sem=recv_sem.at[signals.index(key)],
            device_id=peer[link], device_id_type=MESH,
        )

    def moves(link, dst, src):
        p, h, e, _ = dst
        key = (p, h, e, link == "c")
        size = halves_of(dst)
        if link == "c":
            return [move(p, slot(p, h, e, 0), slot(p, h, e, 1), size, "c", key)]
        if link == "x":
            skip = (SIZE[e] * 2 * PANELS[p][1] - size) // 2
            return [move(p, slot(p, 0, e, 0) + skip, slot(p, 1, e, 0) + skip, size, "x", key)]
        both = []
        for s, way in ((1, "zm"), (-1, "zp")):
            skip = 0 if s == 1 else 2 * PANELS[p][1] - size
            at = slot(p, h, s * (e - 1), 0) + skip
            to = slot(p, h, s * e if e < 4 else 4, 0) + skip
            both.append(move(p, at, to, size, way, key))
        return both

    seen = set()

    def need(p, h, e, twin):
        key = (p, h, e, twin)
        if key in seen:
            return
        seen.add(key)
        if key[1:] == (0, 0, False):
            phase(p)
            return
        ref = group(p, h, e, 1 if twin else 0)
        pltpu.make_async_remote_copy(
            src_ref=ref, dst_ref=ref, send_sem=send_sem.at[p], recv_sem=recv_sem.at[signals.index(key)],
            device_id=peer["c"], device_id_type=MESH,
        ).wait_recv()

    def panel(p):
        return pl.ds(*PANELS[p])

    begun = set()

    def product(p, job, last):
        left, right = [], []
        first, units = PANELS[p]
        for h, e in job:
            for d in (e, -e) if e in (1, 2, 3) else (e,):
                for mine in (0, 1):
                    left.append(got[pl.ds(slot(p, h, d, mine), 2 * units)].reshape(units * 128, 128))
                    chip = (z + d + 8) % 8 * 2 + (xh if h == 0 else 1 - xh)
                    beam = chip * 2 + (core if mine == 0 else 1 - core)
                    right.append(s_ref[:, pl.ds(pl.multiple_of(beam * 128, 128), 128)])
        result = lax.dot_general(
            jnp.concatenate(left, axis=1), jnp.concatenate(right, axis=1), (((1,), (1,)), ((), ())),
            preferred_element_type=jnp.float32,
        )
        mine = pl.ds(first * 128, units * 128)
        if p in begun:
            result += acc[mine]
        begun.add(p)
        if not last:
            acc[mine] = result
            return
        pairs = result.reshape(units * 8, 2, UNIT, 2 * rows)
        re, im = pairs[:, 0], pairs[:, 1]
        both = jnp.stack([re[..., :rows] - im[..., rows:], im[..., :rows] + re[..., rows:]], axis=1)
        both = both.reshape(units, 128, rows)
        total[panel(p)] = both
        part[panel(p)] = both.astype(jnp.bfloat16)

    def y_copy(p, j):
        to = pl.ds(pl.multiple_of((y + j) % 4 * 32, 32), 32)
        return pltpu.make_async_remote_copy(
            src_ref=part.at[panel(p), to], dst_ref=yrecv.at[j - 1, panel(p)],
            send_sem=rs_send.at[p], recv_sem=rs_recv.at[p], device_id=peer[(j, 0)], device_id_type=MESH,
        )

    def x_copy(p):
        return pltpu.make_async_remote_copy(
            src_ref=xsend.at[panel(p)], dst_ref=xrecv.at[panel(p)],
            send_sem=rs_send.at[len(PANELS) + p], recv_sem=rs_recv.at[len(PANELS) + p],
            device_id=peer[(0, 1)], device_id_type=MESH,
        )

    def direct_copy(p, k):
        to = pl.ds(pl.multiple_of(owner[k] * 16, 16), 16)
        return pltpu.make_async_remote_copy(
            src_ref=part.at[panel(p), to], dst_ref=drecv.at[owners.index(k), panel(p)],
            send_sem=rs_send.at[p], recv_sem=rs_recv.at[p], device_id=peer[k], device_id_type=MESH,
        )

    def scattered(p):
        ref = (drecv if p in DIRECT else yrecv).at[:, panel(p)]
        return pltpu.make_async_remote_copy(
            src_ref=ref, dst_ref=ref, send_sem=rs_send.at[p], recv_sem=rs_recv.at[p],
            device_id=peer["c"], device_id_type=MESH,
        )

    def scatter(p):
        if p in DIRECT:
            for k in ((2, 1), (2, 0), (1, 1), (3, 1), (1, 0), (3, 0), (0, 1)):
                direct_copy(p, k).start()
        else:
            for j in (2, 1, 3):
                y_copy(p, j).start()

    def scatter_x(p):
        scattered(p).wait_recv()
        for to in (1, 0):
            which = (xl + to) % 2
            t = total[panel(p), pl.ds(pl.multiple_of(y * 32 + which * 16, 16), 16)]
            for j in range(3):
                t += yrecv[j, panel(p), pl.ds(pl.multiple_of(which * 16, 16), 16)].astype(jnp.float32)
            if to:
                xsend[panel(p)] = t.astype(jnp.bfloat16)
                x_copy(p).start()
            else:
                ysum[panel(p)] = t

    def finish(p):
        if p in DIRECT:
            scattered(p).wait_recv()
            t = total[panel(p), pl.ds(pl.multiple_of(col * 16, 16), 16)]
            for i in range(len(owners)):
                t += drecv[i, panel(p)].astype(jnp.float32)
        else:
            x_copy(p).wait_recv()
            t = ysum[panel(p)] + xrecv[panel(p)].astype(jnp.float32)
        first, units = PANELS[p]
        for u in range(units):
            at = UNIT * (first + u)
            final[0, at:at + UNIT] = t[u, :UNIT]
            final[1, at:at + UNIT] = t[u, UNIT:]

    need(0, 0, 0, False)
    pl.semaphore_wait(barrier, len(peer))
    todo = {p: 10 for p in range(len(PANELS))}
    loaded = False
    for step in ORDER:
        if isinstance(step, int):
            link, dst, src = table[step]
            need(*src, False)
            for c in moves(link, dst, src):
                c.start()
        elif len(step) == 2:
            p, job = step
            for h, e in job:
                need(p, h, e, False)
                need(p, h, e, True)
            if not loaded:
                loaded = True
                for c in s_copies:
                    c.wait()
            todo[p] -= len(job)
            product(p, job, todo[p] == 0)
            if todo[p] == 0:
                scatter(p)
        else:
            scatter_x(step[0])
    for p in range(len(PANELS)):
        sent = sum(halves_of(t[1]) * (2 if t[0] == "z" else 1) for t in table if t[1][0] == p)
        move(p, 0, 0, sent, "c", signals[0]).wait_send()
    for p in range(len(PANELS)):
        finish(p)
    out_ref[...] = final[...].astype(jnp.bfloat16)
    for p in range(len(PANELS)):
        scattered(p).wait_send()
        if p not in DIRECT:
            x_copy(p).wait_send()


def per_device(s_matrix, slab, beam_hkl):
    rows, beams = s_matrix.shape[1:]
    units = sum(PANELS[-1])
    n_signals = len(PANELS) * 19
    out = pl.pallas_call(
        kernel,
        out_shape=pltpu.VMEM((2, units * UNIT, rows), jnp.bfloat16),
        in_specs=[pl.BlockSpec(memory_space=pltpu.HBM)] * 3,
        out_specs=pl.BlockSpec(memory_space=pltpu.VMEM),
        scratch_shapes=[
            pltpu.VMEM((2 * rows, beams), jnp.bfloat16),
            pltpu.VMEM(slab.shape, jnp.bfloat16),
            pltpu.VMEM(beam_hkl.shape, jnp.int32),
            pltpu.VMEM((2, slab.shape[2], slab.shape[1]), jnp.float32),
            pltpu.VMEM((units * 64, 64, 128), jnp.bfloat16),
            pltpu.VMEM((units * 128, 2 * rows), jnp.float32),
            pltpu.VMEM((units, 128, rows), jnp.float32),
            pltpu.VMEM((units, 128, rows), jnp.bfloat16),
            pltpu.VMEM((3, units, 32, rows), jnp.bfloat16),
            pltpu.VMEM((7, units, 16, rows), jnp.bfloat16),
            pltpu.VMEM((units, 16, rows), jnp.float32),
            pltpu.VMEM((units, 16, rows), jnp.bfloat16),
            pltpu.VMEM((units, 16, rows), jnp.bfloat16),
            pltpu.VMEM((2, units * UNIT, rows), jnp.float32),
            pltpu.SemaphoreType.DMA((4,)),
            pltpu.SemaphoreType.DMA((len(PANELS),)),
            pltpu.SemaphoreType.DMA((n_signals,)),
            pltpu.SemaphoreType.DMA((2 * len(PANELS),)),
            pltpu.SemaphoreType.DMA((2 * len(PANELS),)),
        ],
        compiler_params=pltpu.CompilerParams(
            collective_id=0, has_side_effects=True, vmem_limit_bytes=63 * 2**20
        ),
        name="squared",
    )(s_matrix, slab, beam_hkl)
    return jnp.swapaxes(out, 1, 2)


def solution(mesh):
    placed = (P(None, "row", "col"), P(None, ("col", "row"), None), P(None, ("col", "row")))
    return jax.shard_map(
        per_device, mesh=mesh, in_specs=placed, out_specs=P(None, "row", "col"), check_vma=False
    )
```

```python
import jax
import jax.numpy as jnp
from jax import lax
from jax.experimental import pallas as pl
from jax.experimental.pallas import tpu as pltpu
from jax.sharding import PartitionSpec as P

MESH = pl.DeviceIdType.MESH
UNIT = 8
PANELS = ((0, 1), (1, 2), (3, 2), (5, 1))
DIRECT = (1, 2, 3)
OFFSETS = (0, 1, -1, 2, -2, 3, -3, 4)
SIZE = (1, 2, 2, 2, 1)
OVER_Z = ({2: 1.0, 4: 1.0}, {2: 1.0, 4: 1.0}, {2: 1.0, 3: 0.5}, {3: 1.0, 4: 1.0})
ORDER = (
    0, 42, 23, 28, 19, 38, 58, (1, ((0, 0),)), 5, 1, 4, 20, 10, 24, 39, 43, (0, ((0, 1),)), 2, 14, 21, 53, 68, 9,
    49, 11, 15, (0, ((1, 0),)), (2, ((1, 0),)), 40, 6, 30, 29, 33, (0, ((0, 0),)), 7, 59, 3, (0, ((1, 1), (0, 2))),
    50, 26, 22, (2, ((0, 1),)), 12, (1, ((1, 0),)), (2, ((0, 2),)), 34, 41, 44, (1, ((0, 1),)), 31, 54,
    (0, ((0, 3),)), 16, 51, 64, (1, ((1, 1),)), 8, 46, 13, 17, (1, ((0, 3),)), 25, (0, ((1, 2),)), (1, ((0, 2),)),
    47, 48, (2, ((1, 1),)), (0, ((0, 4),)), 27, (3, ((0, 1),)), 52, 45, 62, 60, 36, 63, 69, 18, (0, ((1, 3),)), 65,
    32, 74, 67, (2, ((0, 0), (0, 4))), 35, (0, ((1, 4),)), 37, 55, (1, ((1, 3), (0, 4))), (1, ((1, 2),)), 56,
    (1, ((1, 4),)), 61, 70, 57, (2, ((1, 2),)), 72, 66, 75, (2, ((1, 3), (0, 3))), (2, ((1, 4),)), (3, ((0, 2),)),
    73, (3, ((0, 0), (1, 0), (0, 3))), 71, (3, ((1, 2),)), 76, (0,), (3, ((1, 1), (1, 3))), (3, ((0, 4), (1, 4))),
)


def transfers():
    table = []
    for p in range(len(PANELS)):
        for e in (1, 2, 3, 4):
            table.append(("z", (p, 0, e, "z"), (p, 0, e - 1)))
        for e in range(5):
            share = OVER_Z[p].get(e, 0.0)
            if share > 0:
                table.append(("z", (p, 1, e, "z"), (p, 1, e - 1)))
            if share < 1:
                table.append(("x", (p, 1, e, "x"), (p, 0, e)))
        for h in (0, 1):
            for e in range(5):
                table.append(("c", (p, h, e, "c"), (p, h, e)))
    return table


def halves_of(target):
    p, h, e, link = target
    halves = 2 * PANELS[p][1]
    if link == "c":
        return SIZE[e] * halves
    share = OVER_Z[p].get(e, 0.0) if h else 1.0
    if link == "z":
        return int(halves * share) if e < 4 else halves // 2
    return int(SIZE[e] * halves * (1 - share))


def kernel(s_any, slab_any, hkl_any, out_ref, s_ref, slab_ref, hkl_ref, turned, got, acc, total, part, yrecv, drecv,
           ysum, xsend, xrecv, final, in_sem, send_sem, recv_sem, rs_send, rs_recv):
    row = lax.axis_index("row")
    col = lax.axis_index("col")
    z, xh, core = row // 4, (row // 2) % 2, row % 2
    y, xl = col // 2, col % 2
    rows = s_any.shape[1]
    peer = {
        "zp": ((z + 1) % 8 * 4 + xh * 2 + core, col),
        "zm": ((z + 7) % 8 * 4 + xh * 2 + core, col),
        "x": (z * 4 + (1 - xh) * 2 + core, col),
        "c": (z * 4 + xh * 2 + 1 - core, col),
    }
    owner = {(dy, dx): (y + dy) % 4 * 2 + (xl + dx) % 2 for dy in range(4) for dx in range(2) if dy or dx}
    owners = list(owner)
    for k in owner:
        peer[k] = (row, owner[k])

    slab_copy = pltpu.make_async_copy(slab_any, slab_ref, in_sem.at[0])
    hkl_copy = pltpu.make_async_copy(hkl_any, hkl_ref, in_sem.at[1])
    s_copies = [
        pltpu.make_async_copy(s_any.at[i], s_ref.at[pl.ds(i * rows, rows)], in_sem.at[2 + i]) for i in range(2)
    ]
    slab_copy.start()
    hkl_copy.start()
    barrier = pltpu.get_barrier_semaphore()
    for name in peer:
        pl.semaphore_signal(barrier, inc=1, device_id=peer[name], device_id_type=MESH)

    hkl_copy.wait()
    f = hkl_ref[...].astype(jnp.float32)
    h0, h1, h2 = f[0:1], f[1:2], f[2:3]
    angles = 0.61 * (h0 * h0 + h1 * h1 + h2 * h2) + 0.29 * h0 - 0.17 * h1 + 0.43 * h2
    cosine, sine = jnp.cos(angles), jnp.sin(angles)
    slab_copy.wait()
    for c in s_copies:
        c.start()
    for i in range(2):
        turned[i] = jnp.transpose(slab_ref[i].astype(jnp.float32))

    def slot(p, h, d, mine):
        first, units = PANELS[p]
        return 2 * (first * 32 + (mine * 16 + h * 8 + OFFSETS.index(d)) * units)

    def group(p, h, e, mine):
        return got.at[pl.ds(slot(p, h, e, mine), SIZE[e] * 2 * PANELS[p][1])]

    def phase(p):
        first, units = PANELS[p]
        for u in range(units):
            for o in range(8):
                at = 48 * o + UNIT * (first + u)
                re, im = turned[0, at:at + UNIT], turned[1, at:at + UNIT]
                both = jnp.concatenate([cosine * re - sine * im, cosine * im + sine * re], axis=0)
                got[slot(p, 0, 0, 0) + 2 * u + o // 4, o % 4 * 16:o % 4 * 16 + 16] = both.astype(jnp.bfloat16)

    table = transfers()
    signals = []
    for link, dst, _ in table:
        key = dst[:3] + (link == "c",)
        if key not in signals:
            signals.append(key)

    def move(p, at, to, size, link, key):
        return pltpu.make_async_remote_copy(
            src_ref=got.at[pl.ds(at, size)], dst_ref=got.at[pl.ds(to, size)],
            send_sem=send_sem.at[p], recv_sem=recv_sem.at[signals.index(key)],
            device_id=peer[link], device_id_type=MESH,
        )

    def moves(link, dst, src):
        p, h, e, _ = dst
        key = (p, h, e, link == "c")
        size = halves_of(dst)
        if link == "c":
            return [move(p, slot(p, h, e, 0), slot(p, h, e, 1), size, "c", key)]
        if link == "x":
            skip = (SIZE[e] * 2 * PANELS[p][1] - size) // 2
            return [move(p, slot(p, 0, e, 0) + skip, slot(p, 1, e, 0) + skip, size, "x", key)]
        both = []
        for s, way in ((1, "zm"), (-1, "zp")):
            skip = 0 if s == 1 else 2 * PANELS[p][1] - size
            at = slot(p, h, s * (e - 1), 0) + skip
            to = slot(p, h, s * e if e < 4 else 4, 0) + skip
            both.append(move(p, at, to, size, way, key))
        return both

    seen = set()

    def need(p, h, e, twin):
        key = (p, h, e, twin)
        if key in seen:
            return
        seen.add(key)
        if key[1:] == (0, 0, False):
            phase(p)
            return
        ref = group(p, h, e, 1 if twin else 0)
        pltpu.make_async_remote_copy(
            src_ref=ref, dst_ref=ref, send_sem=send_sem.at[p], recv_sem=recv_sem.at[signals.index(key)],
            device_id=peer["c"], device_id_type=MESH,
        ).wait_recv()

    def panel(p):
        return pl.ds(*PANELS[p])

    begun = set()

    def product(p, job, last):
        left, right = [], []
        first, units = PANELS[p]
        for h, e in job:
            for d in (e, -e) if e in (1, 2, 3) else (e,):
                for mine in (0, 1):
                    left.append(got[pl.ds(slot(p, h, d, mine), 2 * units)].reshape(units * 128, 128))
                    chip = (z + d + 8) % 8 * 2 + (xh if h == 0 else 1 - xh)
                    beam = chip * 2 + (core if mine == 0 else 1 - core)
                    right.append(s_ref[:, pl.ds(pl.multiple_of(beam * 128, 128), 128)])
        result = lax.dot_general(
            jnp.concatenate(left, axis=1), jnp.concatenate(right, axis=1), (((1,), (1,)), ((), ())),
            preferred_element_type=jnp.float32,
        )
        mine = pl.ds(first * 128, units * 128)
        if p in begun:
            result += acc[mine]
        begun.add(p)
        if not last:
            acc[mine] = result
            return
        pairs = result.reshape(units * 8, 2, UNIT, 2 * rows)
        re, im = pairs[:, 0], pairs[:, 1]
        both = jnp.stack([re[..., :rows] - im[..., rows:], im[..., :rows] + re[..., rows:]], axis=1)
        both = both.reshape(units, 128, rows)
        total[panel(p)] = both
        part[panel(p)] = both.astype(jnp.bfloat16)

    def y_copy(p, j):
        to = pl.ds(pl.multiple_of((y + j) % 4 * 32, 32), 32)
        return pltpu.make_async_remote_copy(
            src_ref=part.at[panel(p), to], dst_ref=yrecv.at[j - 1, panel(p)],
            send_sem=rs_send.at[p], recv_sem=rs_recv.at[p], device_id=peer[(j, 0)], device_id_type=MESH,
        )

    def x_copy(p):
        return pltpu.make_async_remote_copy(
            src_ref=xsend.at[panel(p)], dst_ref=xrecv.at[panel(p)],
            send_sem=rs_send.at[len(PANELS) + p], recv_sem=rs_recv.at[len(PANELS) + p],
            device_id=peer[(0, 1)], device_id_type=MESH,
        )

    def direct_copy(p, k):
        to = pl.ds(pl.multiple_of(owner[k] * 16, 16), 16)
        return pltpu.make_async_remote_copy(
            src_ref=part.at[panel(p), to], dst_ref=drecv.at[owners.index(k), panel(p)],
            send_sem=rs_send.at[p], recv_sem=rs_recv.at[p], device_id=peer[k], device_id_type=MESH,
        )

    def scattered(p):
        ref = (drecv if p in DIRECT else yrecv).at[:, panel(p)]
        return pltpu.make_async_remote_copy(
            src_ref=ref, dst_ref=ref, send_sem=rs_send.at[p], recv_sem=rs_recv.at[p],
            device_id=peer["c"], device_id_type=MESH,
        )

    def scatter(p):
        if p in DIRECT:
            for k in ((2, 1), (2, 0), (1, 1), (3, 1), (1, 0), (3, 0), (0, 1)):
                direct_copy(p, k).start()
        else:
            for j in (2, 1, 3):
                y_copy(p, j).start()

    def scatter_x(p):
        scattered(p).wait_recv()
        for to in (1, 0):
            which = (xl + to) % 2
            t = total[panel(p), pl.ds(pl.multiple_of(y * 32 + which * 16, 16), 16)]
            for j in range(3):
                t += yrecv[j, panel(p), pl.ds(pl.multiple_of(which * 16, 16), 16)].astype(jnp.float32)
            if to:
                xsend[panel(p)] = t.astype(jnp.bfloat16)
                x_copy(p).start()
            else:
                ysum[panel(p)] = t

    def finish(p):
        if p in DIRECT:
            scattered(p).wait_recv()
            t = total[panel(p), pl.ds(pl.multiple_of(col * 16, 16), 16)]
            for i in range(len(owners)):
                t += drecv[i, panel(p)].astype(jnp.float32)
        else:
            x_copy(p).wait_recv()
            t = ysum[panel(p)] + xrecv[panel(p)].astype(jnp.float32)
        first, units = PANELS[p]
        for u in range(units):
            at = UNIT * (first + u)
            final[0, at:at + UNIT] = t[u, :UNIT]
            final[1, at:at + UNIT] = t[u, UNIT:]

    need(0, 0, 0, False)
    pl.semaphore_wait(barrier, len(peer))
    todo = {p: 10 for p in range(len(PANELS))}
    loaded = False
    for step in ORDER:
        if isinstance(step, int):
            link, dst, src = table[step]
            need(*src, False)
            for c in moves(link, dst, src):
                c.start()
        elif len(step) == 2:
            p, job = step
            for h, e in job:
                need(p, h, e, False)
                need(p, h, e, True)
            if not loaded:
                loaded = True
                for c in s_copies:
                    c.wait()
            todo[p] -= len(job)
            product(p, job, todo[p] == 0)
            if todo[p] == 0:
                scatter(p)
        else:
            scatter_x(step[0])
    for p in range(len(PANELS)):
        sent = sum(halves_of(t[1]) * (2 if t[0] == "z" else 1) for t in table if t[1][0] == p)
        move(p, 0, 0, sent, "c", signals[0]).wait_send()
    for p in range(len(PANELS)):
        finish(p)
    out_ref[...] = final[...].astype(jnp.bfloat16)
    for p in range(len(PANELS)):
        scattered(p).wait_send()
        if p not in DIRECT:
            x_copy(p).wait_send()


def per_device(s_matrix, slab, beam_hkl):
    rows, beams = s_matrix.shape[1:]
    units = sum(PANELS[-1])
    n_signals = len(PANELS) * 19
    out = pl.pallas_call(
        kernel,
        out_shape=pltpu.VMEM((2, units * UNIT, rows), jnp.bfloat16),
        in_specs=[pl.BlockSpec(memory_space=pltpu.HBM)] * 3,
        out_specs=pl.BlockSpec(memory_space=pltpu.VMEM),
        scratch_shapes=[
            pltpu.VMEM((2 * rows, beams), jnp.bfloat16),
            pltpu.VMEM(slab.shape, jnp.bfloat16),
            pltpu.VMEM(beam_hkl.shape, jnp.int32),
            pltpu.VMEM((2, slab.shape[2], slab.shape[1]), jnp.float32),
            pltpu.VMEM((units * 64, 64, 128), jnp.bfloat16),
            pltpu.VMEM((units * 128, 2 * rows), jnp.float32),
            pltpu.VMEM((units, 128, rows), jnp.float32),
            pltpu.VMEM((units, 128, rows), jnp.bfloat16),
            pltpu.VMEM((3, units, 32, rows), jnp.bfloat16),
            pltpu.VMEM((7, units, 16, rows), jnp.bfloat16),
            pltpu.VMEM((units, 16, rows), jnp.float32),
            pltpu.VMEM((units, 16, rows), jnp.bfloat16),
            pltpu.VMEM((units, 16, rows), jnp.bfloat16),
            pltpu.VMEM((2, units * UNIT, rows), jnp.float32),
            pltpu.SemaphoreType.DMA((4,)),
            pltpu.SemaphoreType.DMA((len(PANELS),)),
            pltpu.SemaphoreType.DMA((n_signals,)),
            pltpu.SemaphoreType.DMA((2 * len(PANELS),)),
            pltpu.SemaphoreType.DMA((2 * len(PANELS),)),
        ],
        compiler_params=pltpu.CompilerParams(
            collective_id=0, has_side_effects=True, vmem_limit_bytes=63 * 2**20
        ),
        name="squared",
    )(s_matrix, slab, beam_hkl)
    return jnp.swapaxes(out, 1, 2)


def solution(mesh):
    placed = (P(None, "row", "col"), P(None, ("col", "row"), None), P(None, ("col", "row")))
    return jax.shard_map(
        per_device, mesh=mesh, in_specs=placed, out_specs=P(None, "row", "col"), check_vma=False
    )
```
